128 devices in a mesh: layer: 4 (over x_hi, core), feat: 16 (over z, y), par: 2 (over x_lo).
Axes of the slice: x: 4 (x_hi: 2, x_lo: 2; x = x_hi * 2 + x_lo), y: 4, z: 4, core: 2. Of those that a mesh axis runs over, the one named last changes fastest.
Arguments:
- residual: bfloat16 [4, 512, 2304], P('layer'), may hold values from -6 to 6
- norm_gain: float32 [4, 2304], P('layer'), may hold values from 0.5 to 1.5
- gate_weight: bfloat16 [4, 2304, 9216], P('layer', None, ('feat', 'par')), may hold values from -0.125 to 0.125
- up_weight: bfloat16 [4, 2304, 9216], P('layer', None, ('feat', 'par')), may hold values from -0.125 to 0.125
- down_weight: bfloat16 [4, 9216, 2304], P('layer', ('feat', 'par')), may hold values from -0.0625 to 0.0625
- enc_weight: float32 [4, 2304, 8192], P('layer', 'par', 'feat'), may hold values from -0.125 to 0.125
- enc_bias: float32 [4, 8192], P('layer', 'feat'), may hold values from -1 to 0.5
- dec_weight: bfloat16 [4, 2, 2, 8192, 2304], P('layer', 'par', None, 'feat'), may hold values from -0.0625 to 0.0625
- dec_bias: float32 [4, 2304], replicated, may hold values from -3 to 3
Outputs:
- enc_grad: float32 [4, 2304, 8192], P('layer', 'par', 'feat')
- enc_bias_grad: float32 [4, 8192], P('layer', 'feat')
- dec_grad: bfloat16 [4, 2, 2, 8192, 2304], P('layer', 'par', None, 'feat')
The draws below stay inside these ranges and needn't reach their ends.
All inputs are finite; a program needn't handle non-finite values.
Results may differ from the reference program's by a relative error of at most 0.007.
Values may be sent and summed in bfloat16 or wider, within the bound.
A program may use at most 192 MiB of HBM per device.

```python
import jax
import jax.numpy as jnp
from jax import lax

D = 2304
FF = 9216
FEATS = 8192
LAYERS = 4
TOKENS = 512


def block_levels(own_key, dims, pieces, low, high):
    factor_of, own = 1.0, jax.random.fold_in(own_key, 6)
    for dim, blocks in pieces:
        draws = jnp.exp(jax.random.uniform(jax.random.fold_in(own, dim), (blocks,), jnp.float32, low / len(pieces), high / len(pieces)))
        factor_of = factor_of * jnp.repeat(draws, dims[dim] // blocks).reshape([-1 if axis == dim else 1 for axis in range(len(dims))])
    return factor_of


def bell_draw(key, shape, scale, reach, split=(), dtype=jnp.bfloat16):
    entries = jax.random.normal(key, shape, jnp.float32) * scale
    if len(split) > 0:
        entries = block_levels(key, shape, split, -0.22, 0.18) * entries
    return jnp.clip(entries, min=-reach, max=reach).astype(dtype)


def setup_inputs(seed: int = 0) -> dict:
    streams_of = jax.random.split(jax.random.key(seed), 10)
    residual = bell_draw(streams_of[0], (LAYERS, TOKENS, D), 1.0, 6.0, ((0, 4),))
    norm_gain = jnp.clip(1.0 + 0.1 * jax.random.normal(streams_of[1], (LAYERS, D), jnp.float32), 0.5, 1.5)
    gate_weight = bell_draw(streams_of[2], (LAYERS, D, FF), D ** -0.5, 0.125, ((0, 4), (2, 32)))
    up_weight = bell_draw(streams_of[3], (LAYERS, D, FF), D ** -0.5, 0.125, ((0, 4), (2, 32)))
    down_weight = bell_draw(streams_of[4], (LAYERS, FF, D), FF ** -0.5, 0.0625, ((0, 4), (1, 32)))
    enc_weight = bell_draw(streams_of[5], (LAYERS, D, FEATS), D ** -0.5, 0.125, ((0, 4), (1, 2), (2, 16)), jnp.float32)
    enc_bias = jnp.clip(-1.0 + 1.5 * jax.random.uniform(streams_of[6], (LAYERS, FEATS), jnp.float32) ** block_levels(streams_of[6], (LAYERS, FEATS), ((0, 4), (1, 16)), -0.2, 0.2), -1.0, 0.5)
    dec_weight = bell_draw(streams_of[7], (LAYERS, 2, LAYERS // 2, FEATS, D), FEATS ** -0.5, 0.0625, ((0, 4), (1, 2), (3, 16)))
    dec_bias = bell_draw(streams_of[8], (LAYERS, D), 0.5, 3.0, (), jnp.float32)
    return {"residual": residual, "norm_gain": norm_gain, "gate_weight": gate_weight, "up_weight": up_weight, "down_weight": down_weight, "enc_weight": enc_weight, "enc_bias": enc_bias, "dec_weight": dec_weight, "dec_bias": dec_bias}


def rms_normed(rows_in, gain_row):
    values = rows_in.astype(jnp.float32)
    scaling = lax.rsqrt(lax.optimization_barrier(jnp.mean(values * values, axis=-1, keepdims=True)) + 1e-06)
    return (values * scaling * gain_row).astype(jnp.bfloat16)

def reference(residual, norm_gain, gate_weight, up_weight, down_weight, enc_weight, enc_bias, dec_weight, dec_bias):
    highest = lax.Precision.HIGHEST
    normed = []
    targets = []
    positives = []
    actives = []
    for source in range(LAYERS):
        rows_in = rms_normed(residual[source], norm_gain[source])
        gate_value = jnp.dot(rows_in, gate_weight[source], preferred_element_type=jnp.float32)
        up_value = jnp.dot(rows_in, up_weight[source], preferred_element_type=jnp.float32)
        hidden = (jax.nn.gelu(gate_value, approximate=True) * up_value).astype(jnp.bfloat16)
        targets.append(jnp.dot(hidden, down_weight[source], preferred_element_type=jnp.float32))
        pre_act = jnp.dot(rows_in.astype(jnp.float32), enc_weight[source], precision=highest) + enc_bias[source]
        positive = jnp.maximum(pre_act, 0.0)
        normed.append(rows_in)
        positives.append(positive)
        actives.append((positive * positive).astype(jnp.bfloat16))
    errors = []
    for target in range(LAYERS):
        summed_rows = jnp.zeros((TOKENS, D), jnp.float32)
        for source in range(target + 1):
            summed_rows = summed_rows + jnp.dot(actives[source], dec_weight[source, target % 2, target // 2], preferred_element_type=jnp.float32)
        errors.append(((summed_rows + dec_bias[target] - targets[target]) * 0.0625).astype(jnp.bfloat16))
    enc_grads = []
    bias_grads = []
    dec_grads = []
    zero_block = jnp.zeros((FEATS, D), jnp.bfloat16)
    for source in range(LAYERS):
        back_grad = jnp.zeros((TOKENS, FEATS), jnp.float32)
        for parity in range(2):
            for slot_index in range(LAYERS // 2):
                target = 2 * slot_index + parity
                if target >= source:
                    back_grad = back_grad + lax.dot_general(errors[target], dec_weight[source, parity, slot_index], (((1,), (1,)), ((), ())), preferred_element_type=jnp.float32)
                    dec_grads.append(lax.dot_general(actives[source], errors[target], (((0,), (0,)), ((), ())), preferred_element_type=jnp.float32).astype(jnp.bfloat16))
                else:
                    dec_grads.append(zero_block)
        d_pre = back_grad * 2.0 * positives[source]
        enc_grads.append(lax.dot_general(normed[source].astype(jnp.float32), d_pre, (((0,), (0,)), ((), ())), precision=highest))
        bias_grads.append(lax.optimization_barrier(jnp.sum(d_pre, axis=0)))
    dec_grad = jnp.stack(dec_grads).reshape(LAYERS, 2, LAYERS // 2, FEATS, D)
    return (jnp.stack(enc_grads), jnp.stack(bias_grads), dec_grad)
```

```python
import jax
import jax.numpy as jnp
from jax import lax
from jax.experimental import pallas as pl
from jax.experimental.pallas import tpu as pltpu
from jax.sharding import PartitionSpec as P

F32 = jnp.float32
BF16 = jnp.bfloat16
MESH = pl.DeviceIdType.MESH

T = 512
D = 2304
W = D // 2
F = 512
U = 288
Q1 = T // 4
Q2 = T // 16
CT = 384
RT = 256


def kernel(
    res_h, gain_v, gate_h, up_h, down_h, enc_h, ebias_v, dec_h, dbias_v,
    egrad_h, bgrad_v, dgrad_h,
    nrm, gate_v, up_v, down_v, hid, enc_v, enc_b, dec_v,
    pre_snd, pre_rcv, pos, act, act_t, acc,
    own, cs_snd, cs_rcv, r1_snd, r1_rcv, r2_snd, r2_rcv, x_snd, x_rcv, fin,
    err, back, bk_snd, bk_rcv, dpre, dg_v,
    ld_sem, out_sem, pre_s, pre_r, hd_s, hd_r, cs_s, cs_r, r1_s, r1_r, r2_s, r2_r, x_s, x_r,
    ga_s, ga_r, gb_s, gb_r, gc_s, gc_r, bk_s, bk_r,
):
    layer = lax.axis_index("layer")
    feat = lax.axis_index("feat")
    par = lax.axis_index("par")
    core = lax.rem(layer, 2)
    x_hi = lax.div(layer, 2)
    zz = lax.div(feat, 4)
    yy = lax.rem(feat, 4)
    a = zz + core * (yy - zz)
    b = yy + core * (zz - yy)
    home = core == par

    def at(first, second):
        return first * 4 + second + core * 3 * (second - first)

    par_id = (layer, feat, 1 - par)
    sib_id = (layer + 1 - 2 * core, feat, par)
    xhi_id = (lax.rem(layer + 2, 4), feat, par)
    step = [None] + [lax.rem(a + k, 4) for k in (1, 2, 3)]
    hop = [None] + [lax.rem(b + k, 4) for k in (1, 2, 3)]
    first_id = [None] + [(layer, at(step[k], b), par) for k in (1, 2, 3)]
    second_id = [None] + [(layer, at(a, hop[k]), par) for k in (1, 2, 3)]

    def remote(src, dst, s, r, to):
        return pltpu.make_async_remote_copy(
            src_ref=src, dst_ref=dst, send_sem=s, recv_sem=r, device_id=to, device_id_type=MESH
        )

    barrier = pltpu.get_barrier_semaphore()
    for to in [par_id, sib_id, xhi_id] + first_id[1:] + second_id[1:]:
        pl.semaphore_signal(barrier, inc=1, device_id=to, device_id_type=MESH)

    loads = [
        pltpu.make_async_copy(res_h.at[0], nrm, ld_sem.at[0]),
        pltpu.make_async_copy(enc_h.at[0], enc_v, ld_sem.at[1]),
        pltpu.make_async_copy(gate_h.at[0], gate_v, ld_sem.at[2]),
        pltpu.make_async_copy(up_h.at[0], up_v, ld_sem.at[3]),
        pltpu.make_async_copy(down_h.at[0], down_v.at[0], ld_sem.at[4]),
        pltpu.make_async_copy(dec_h.at[0, 0], dec_v, ld_sem.at[5]),
    ]
    for load in loads:
        load.start()

    loads[0].wait()

    def norm_rows(i, _):
        rows = pl.ds(pl.multiple_of(i * 32, 32), 32)
        x = nrm[rows, :].astype(F32)
        scale = lax.rsqrt(jnp.mean(x * x, axis=-1, keepdims=True) + 1e-6)
        nrm[rows, :] = (x * scale * gain_v[...]).astype(BF16)
        return 0

    lax.fori_loop(0, T // 32, norm_rows, 0)
    loads[1].wait()

    def enc_rows(i, _):
        rows = pl.ds(pl.multiple_of(i * 128, 128), 128)
        enc_b[rows, :] = enc_v[rows, :].astype(BF16)
        return 0

    lax.fori_loop(0, W // 128, enc_rows, 0)
    my_cols = pl.ds(pl.multiple_of(par * W, W), W)

    pl.semaphore_wait(barrier, 9)
    pre_copy = []
    for c in range(2):
        rows = pl.ds(c * RT, RT)
        part = jnp.dot(nrm[rows, my_cols], enc_b[...], preferred_element_type=F32)
        pos[rows, :] = part
        pre_snd[rows, :] = part.astype(BF16)
        pre_copy.append(remote(pre_snd.at[rows], pre_rcv.at[rows], pre_s.at[c], pre_r.at[c], par_id))
        pre_copy[c].start()

    loads[4].wait()
    down_copy = remote(down_v.at[0], down_v.at[1], hd_s.at[0], hd_r.at[0], par_id)
    hid_copy = remote(hid.at[0], hid.at[1], hd_s.at[1], hd_r.at[1], par_id)

    @pl.when(jnp.logical_not(home))
    def _():
        down_copy.start()

    loads[2].wait()
    loads[3].wait()

    def mlp_rows(i, _):
        rows = pl.ds(pl.multiple_of(i * RT, RT), RT)
        g = jnp.dot(nrm[rows, :], gate_v[...], preferred_element_type=F32)
        u = jnp.dot(nrm[rows, :], up_v[...], preferred_element_type=F32)
        inner = 0.7978845608028654 * (g + 0.044715 * g * g * g)
        hid[0, rows, :] = (0.5 * g * (1.0 + jnp.tanh(inner)) * u).astype(BF16)
        return 0

    lax.fori_loop(0, T // RT, mlp_rows, 0)

    @pl.when(jnp.logical_not(home))
    def _():
        hid_copy.start()

    for c in range(2):
        pre_copy[c].wait_recv()

        def act_rows(i, _):
            rows = pl.ds(pl.multiple_of(c * RT + i * 32, 32), 32)
            p = jnp.maximum(pos[rows, :] + pre_rcv[rows, :].astype(F32) + ebias_v[...], 0.0)
            pos[rows, :] = p
            act[rows, :] = (p * p).astype(BF16)
            return 0

        lax.fori_loop(0, RT // 32, act_rows, 0)
    loads[5].wait()

    slots = [1 - x_hi, x_hi]
    wave_copy = [None, None]

    def recon_tiles(k, half, r, to_sibling):
        j = slots[k]
        live = (2 * j + par >= layer).astype(F32)
        rows = pl.ds(r * RT, RT)

        def tile(n, _):
            local = pl.ds(pl.multiple_of(n * CT, CT), CT)
            cols = pl.ds(pl.multiple_of(half * W + n * CT, CT), CT)
            acc[...] = jnp.dot(act[rows, :], dec_v[j, :, cols], preferred_element_type=F32) * live
            if k == 1:

                @pl.when(home)
                def _():
                    acc[...] -= jnp.dot(
                        hid[0, rows, :], down_v[0, :, cols], preferred_element_type=F32
                    ) + jnp.dot(hid[1, rows, :], down_v[1, :, cols], preferred_element_type=F32)

            if to_sibling:
                cs_snd[k, rows, local] = acc[...].astype(BF16)
            else:
                own[k, rows, local] = acc[...]
            return 0

        lax.fori_loop(0, W // CT, tile, 0)

    def produce(k):
        copies = []
        for r in range(2):
            recon_tiles(k, 1 - core, r, True)
            rows = pl.ds(r * RT, RT)
            copies.append(
                remote(cs_snd.at[k, rows], cs_rcv.at[k, rows], cs_s.at[k, r], cs_r.at[k, r], sib_id)
            )
            copies[r].start()
        for r in range(2):
            recon_tiles(k, core, r, False)
        return copies

    def scatter_first(k, pair):
        for copy in pair:
            copy.wait_recv()
        copies = [None]
        for n in (1, 2, 3):

            def add_rows(i, _):
                rows = pl.ds(pl.multiple_of(step[n] * Q1 + i * 32, 32), 32)
                here = pl.ds(pl.multiple_of(i * 32, 32), 32)
                r1_snd[k, n - 1, here, :] = (own[k, rows, :] + cs_rcv[k, rows, :].astype(F32)).astype(BF16)
                return 0

            lax.fori_loop(0, Q1 // 32, add_rows, 0)
            copies.append(
                remote(r1_snd.at[k, n - 1], r1_rcv.at[k, n - 1], r1_s.at[k, n - 1], r1_r.at[k, n - 1], first_id[n])
            )
            copies[n].start()
        return copies

    def sum_first(k, q, _):
        rows = pl.ds(pl.multiple_of(a * Q1 + q * Q2, Q2), Q2)
        here = pl.ds(pl.multiple_of(q * Q2, Q2), Q2)
        total = own[k, rows, :] + cs_rcv[k, rows, :].astype(F32)
        for n in range(3):
            total = total + r1_rcv[k, n, here, :].astype(F32)
        return total

    def scatter_second(k, arrived):
        for n in (1, 2, 3):
            arrived[n].wait_recv()
        copies = [None]
        for n in (1, 2, 3):
            r2_snd[k, n - 1] = sum_first(k, hop[n], 0).astype(BF16)
            copies.append(
                remote(r2_snd.at[k, n - 1], r2_rcv.at[k, n - 1], r2_s.at[k, n - 1], r2_r.at[k, n - 1], second_id[n])
            )
            copies[n].start()
        fin[k] = sum_first(k, b, 0)
        return copies

    def finish(k, arrived):
        for n in (1, 2, 3):
            arrived[n].wait_recv()
        total = fin[k]
        for n in range(3):
            total = total + r2_rcv[k, n].astype(F32)
        fin[k] = total

    x_copy = remote(x_snd, x_rcv, x_s, x_r, xhi_id)

    def send_x(k):
        x_snd[...] = fin[k].astype(BF16)
        x_copy.start()

    low = x_hi == 0

    pair1 = [None]
    @pl.when(low)
    def _():
        pair = produce(0)
        scatter_first(0, pair)

    first0 = [None] + [
        remote(r1_snd.at[0, n - 1], r1_rcv.at[0, n - 1], r1_s.at[0, n - 1], r1_r.at[0, n - 1], first_id[n])
        for n in (1, 2, 3)
    ]

    act_t[...] = act[...].T

    @pl.when(home)
    def _():
        down_copy.wait_recv()
        hid_copy.wait_recv()

    pair1 = produce(1)

    @pl.when(low)
    def _():
        second = scatter_second(0, first0)

    first1 = scatter_first(1, pair1)

    @pl.when(low)
    def _():
        second = [None] + [
            remote(r2_snd.at[0, n - 1], r2_rcv.at[0, n - 1], r2_s.at[0, n - 1], r2_r.at[0, n - 1], second_id[n])
            for n in (1, 2, 3)
        ]
        finish(0, second)
        send_x(0)

    second1 = scatter_second(1, first1)
    finish(1, second1)

    @pl.when(jnp.logical_not(low))
    def _():
        send_x(1)

    half_cols = pl.ds(pl.multiple_of(core * W, W), W)
    my_rows = pl.ds(pl.multiple_of(a * Q1 + b * Q2, Q2), Q2)

    def write_error(j, total):
        bias = dbias_v[pl.ds(2 * j + par, 1), half_cols]
        err[core, j, my_rows, :] = ((total + bias) * 0.0625).astype(BF16)

    def gather_a(j, n):
        piece = err.at[core, j, my_rows]
        return remote(piece, piece, ga_s.at[j, n - 1], ga_r.at[j, n - 1], second_id[n])

    def block(first):
        return pl.ds(pl.multiple_of(first * Q1, Q1), Q1)

    def gather_b(j, n):
        piece = err.at[core, j, block(a)]
        return remote(piece, piece, gb_s.at[j, n - 1], gb_r.at[j, n - 1], first_id[n])

    def gather_c(j, n):
        piece = err.at[core, j, block(lax.rem(a + 4 - n, 4))]
        return remote(piece, piece, gc_s.at[j, n], gc_r.at[j, n], sib_id)

    def run_gather_a(j):
        for n in (1, 2, 3):
            gather_a(j, n).start()

    def run_gather_b(j):
        for n in (1, 2, 3):
            gather_a(j, n).wait_recv()
        for n in (1, 2, 3):
            gather_b(j, n).start()
        gather_c(j, 0).start()

    def run_gather_c(j):
        for n in (1, 2, 3):
            gather_b(j, n).wait_recv()
            gather_c(j, n).start()

    def wait_error(j):
        for n in range(4):
            rows = block(lax.rem(b + 4 - n, 4))
            remote(
                err.at[1 - core, j, rows], err.at[1 - core, j, rows], gc_s.at[j, n], gc_r.at[j, n], sib_id
            ).wait_recv()

    @pl.when(low)
    def _():
        write_error(0, fin[1])
        run_gather_a(0)

    x_copy.wait_recv()

    write_error(1, lax.select(jnp.broadcast_to(low, (Q2, W)), fin[0], fin[1]) + x_rcv[...].astype(F32))
    run_gather_a(1)

    @pl.when(low)
    def _():
        run_gather_b(0)

    run_gather_b(1)

    @pl.when(low)
    def _():
        run_gather_c(0)
        wait_error(0)

    live0 = par >= layer
    live1 = 2 + par >= layer

    def back_tile(j, r):
        rows = pl.ds(r * RT, RT)
        out = None
        for h in range(2):
            term = lax.dot_general(
                err[h, j, rows, :], dec_v[j, :, pl.ds(h * W, W)], (((1,), (1,)), ((), ())),
                preferred_element_type=F32,
            )
            out = term if out is None else out + term
        return out

    def dec_grad(j):
        def tile(n, _):
            for h in range(2):
                for m in range(2):
                    local = pl.ds(pl.multiple_of(n * CT, CT), CT)
                    cols = pl.ds(pl.multiple_of(h * W + n * CT, CT), CT)
                    rows = pl.ds(m * RT, RT)
                    dg_v[j, rows, cols] = jnp.dot(
                        act_t[rows, :], err[h, j, :, local], preferred_element_type=F32
                    ).astype(BF16)
            return 0

        lax.fori_loop(0, W // CT, tile, 0)

    def no_dec_grad(j):
        def rows_of(i, _):
            rows = pl.ds(pl.multiple_of(i * 32, 32), 32)
            dg_v[j, rows, :] = jnp.zeros((32, D), BF16)
            return 0

        lax.fori_loop(0, F // 32, rows_of, 0)

    outs = [pltpu.make_async_copy(dg_v.at[j], dgrad_h.at[0, 0, j], out_sem.at[j]) for j in range(2)]

    @pl.when(live0)
    def _():
        for r in range(2):
            back[pl.ds(r * RT, RT), :] = back_tile(0, r)
        dec_grad(0)

    @pl.when(jnp.logical_not(live0))
    def _():
        back[...] = jnp.zeros((T, F), F32)
        no_dec_grad(0)

    outs[0].start()
    run_gather_c(1)
    wait_error(1)

    bk_copy = []
    for r in range(2):
        rows = pl.ds(r * RT, RT)

        @pl.when(live1)
        def _():
            back[rows, :] += back_tile(1, r)

        bk_snd[rows, :] = back[rows, :].astype(BF16)
        bk_copy.append(remote(bk_snd.at[rows], bk_rcv.at[rows], bk_s.at[r], bk_r.at[r], par_id))
        bk_copy[r].start()

    @pl.when(live1)
    def _():
        dec_grad(1)

    @pl.when(jnp.logical_not(live1))
    def _():
        no_dec_grad(1)

    outs[1].start()

    bgrad_v[...] = jnp.zeros((1, F), F32)
    for r in range(2):
        bk_copy[r].wait_recv()

        def dpre_rows(i, _):
            rows = pl.ds(pl.multiple_of(r * RT + i * 32, 32), 32)
            d = (back[rows, :] + bk_rcv[rows, :].astype(F32)) * 2.0 * pos[rows, :]
            dpre[rows, :] = d.astype(BF16)
            bgrad_v[...] += jnp.sum(d, axis=0, keepdims=True)
            return 0

        lax.fori_loop(0, RT // 32, dpre_rows, 0)

    for n in range(W // CT):
        cols = pl.ds(pl.multiple_of(par * W + n * CT, 128), CT)
        enc_v[pl.ds(n * CT, CT), :] = lax.dot_general(
            nrm[:, cols], dpre[...], (((0,), (0,)), ((), ())), preferred_element_type=F32
        )
    last = pltpu.make_async_copy(enc_v, egrad_h.at[0], out_sem.at[2])
    last.start()

    for c in range(2):
        pre_copy[c].wait_send()
        bk_copy[c].wait_send()
        pair1[c].wait_send()

    @pl.when(jnp.logical_not(home))
    def _():
        down_copy.wait_send()
        hid_copy.wait_send()

    x_copy.wait_send()
    for n in (1, 2, 3):
        first1[n].wait_send()
        second1[n].wait_send()
        gather_a(1, n).wait_send()
        gather_b(1, n).wait_send()
    for n in range(4):
        gather_c(1, n).wait_send()

    @pl.when(low)
    def _():
        for r in range(2):
            rows = pl.ds(r * RT, RT)
            remote(cs_snd.at[0, rows], cs_rcv.at[0, rows], cs_s.at[0, r], cs_r.at[0, r], sib_id).wait_send()
        for n in (1, 2, 3):
            first0[n].wait_send()
            remote(
                r2_snd.at[0, n - 1], r2_rcv.at[0, n - 1], r2_s.at[0, n - 1], r2_r.at[0, n - 1], second_id[n]
            ).wait_send()
            gather_a(0, n).wait_send()
            gather_b(0, n).wait_send()
        for n in range(4):
            gather_c(0, n).wait_send()

    for copy in outs:
        copy.wait()
    last.wait()


def shards(
    residual, norm_gain, gate_weight, up_weight, down_weight, enc_weight, enc_bias, dec_weight, dec_bias
):
    any_spec = pl.BlockSpec(memory_space=pl.ANY)
    vmem = pl.BlockSpec(memory_space=pltpu.VMEM)
    dma = pltpu.SemaphoreType.DMA
    scratch = [
        pltpu.VMEM((T, D), BF16),
        pltpu.VMEM((D, U), BF16),
        pltpu.VMEM((D, U), BF16),
        pltpu.VMEM((2, U, D), BF16),
        pltpu.VMEM((2, T, U), BF16),
        pltpu.VMEM((W, F), F32),
        pltpu.VMEM((W, F), BF16),
        pltpu.VMEM((2, F, D), BF16),
        pltpu.VMEM((T, F), BF16),
        pltpu.VMEM((T, F), BF16),
        pltpu.VMEM((T, F), F32),
        pltpu.VMEM((T, F), BF16),
        pltpu.VMEM((F, T), BF16),
        pltpu.VMEM((RT, CT), F32),
        pltpu.VMEM((2, T, W), F32),
        pltpu.VMEM((2, T, W), BF16),
        pltpu.VMEM((2, T, W), BF16),
        pltpu.VMEM((2, 3, Q1, W), BF16),
        pltpu.VMEM((2, 3, Q1, W), BF16),
        pltpu.VMEM((2, 3, Q2, W), BF16),
        pltpu.VMEM((2, 3, Q2, W), BF16),
        pltpu.VMEM((Q2, W), BF16),
        pltpu.VMEM((Q2, W), BF16),
        pltpu.VMEM((2, Q2, W), F32),
        pltpu.VMEM((2, 2, T, W), BF16),
        pltpu.VMEM((T, F), F32),
        pltpu.VMEM((T, F), BF16),
        pltpu.VMEM((T, F), BF16),
        pltpu.VMEM((T, F), BF16),
        pltpu.VMEM((2, F, D), BF16),
        dma((6,)), dma((3,)),
        dma((2,)), dma((2,)),
        dma((2,)), dma((2,)),
        dma((2, 2)), dma((2, 2)),
        dma((2, 3)), dma((2, 3)),
        dma((2, 3)), dma((2, 3)),
        dma, dma,
        dma((2, 3)), dma((2, 3)),
        dma((2, 3)), dma((2, 3)),
        dma((2, 4)), dma((2, 4)),
        dma((2,)), dma((2,)),
    ]
    return pl.pallas_call(
        kernel,
        out_shape=(
            jax.ShapeDtypeStruct((1, W, F), F32),
            jax.ShapeDtypeStruct((1, F), F32),
            jax.ShapeDtypeStruct((1, 1, 2, F, D), BF16),
        ),
        in_specs=[any_spec, vmem, any_spec, any_spec, any_spec, any_spec, vmem, any_spec, vmem],
        out_specs=(any_spec, vmem, any_spec),
        scratch_shapes=scratch,
        compiler_params=pltpu.CompilerParams(
            collective_id=0, has_side_effects=True, vmem_limit_bytes=62 * 1024 * 1024
        ),
    )(residual, norm_gain, gate_weight, up_weight, down_weight, enc_weight, enc_bias, dec_weight, dec_bias)


def solution(mesh):
    return jax.shard_map(
        shards,
        mesh=mesh,
        in_specs=(
            P("layer", None, None),
            P("layer", None),
            P("layer", None, ("feat", "par")),
            P("layer", None, ("feat", "par")),
            P("layer", ("feat", "par"), None),
            P("layer", "par", "feat"),
            P("layer", "feat"),
            P("layer", "par", None, "feat", None),
            P(),
        ),
        out_specs=(
            P("layer", "par", "feat"),
            P("layer", "feat"),
            P("layer", "par", None, "feat", None),
        ),
        check_vma=False,
    )
```

```python
import jax
import jax.numpy as jnp
from jax import lax
from jax.experimental import pallas as pl
from jax.experimental.pallas import tpu as pltpu
from jax.sharding import PartitionSpec as P

F32 = jnp.float32
BF16 = jnp.bfloat16
MESH = pl.DeviceIdType.MESH

T = 512
D = 2304
W = D // 2
F = 512
U = 288
Q1 = T // 4
QH = Q1 // 2
Q2 = T // 16
CT = 384
RT = 256
BT = 128


def kernel(
    res_h, gain_v, gate_h, up_h, down_h, enc_h, ebias_v, dec_h, dbias_v,
    rows_h, dpre_h, bgrad_v, dgrad_h,
    nrm, rows_t, gate_v, up_v, down_v, hid, enc_v, enc_b, dec_v,
    pre_snd, pre_rcv, pos, act, act_t,
    own, cs_snd, cs_rcv, part, relay, r1_rcv, r2_snd, r2_rcv, fin, tg_snd, tg_rcv, x_snd, x_rcv,
    err, back, bk_snd, bk_rcv, dpre, dg_v,
    ld_sem, out_sem, pre_s, pre_r, cs_s, cs_r, r1_s, r1_r, r2_s, r2_r, tg_s, tg_r, x_s, x_r,
    ga_s, ga_r, gb_s, gb_r, gc_s, gc_r, bk_s, bk_r,
):
    layer = lax.axis_index("layer")
    feat = lax.axis_index("feat")
    par = lax.axis_index("par")
    core = lax.rem(layer, 2)
    x_hi = lax.div(layer, 2)
    zz = lax.div(feat, 4)
    yy = lax.rem(feat, 4)
    low = x_hi == 0
    home = core == par
    away = core != par

    def first_of(role):
        return zz + role * (yy - zz)

    def second_of(role):
        return yy + role * (zz - yy)

    def at(role, first, second):
        return (layer, first * 4 + second + role * 3 * (second - first), par)

    def turn(x, n):
        return lax.rem(x + n, 4)

    sib = layer + 1 - 2 * core
    par_id = (layer, feat, 1 - par)
    sib_id = (sib, feat, par)
    diag_id = (sib, feat, 1 - par)
    xhi_id = (turn(layer, 2), feat, par)

    def remote(src, dst, s, r, to):
        return pltpu.make_async_remote_copy(
            src_ref=src, dst_ref=dst, send_sem=s, recv_sem=r, device_id=to, device_id_type=MESH
        )

    barrier = pltpu.get_barrier_semaphore()
    peers = [par_id, sib_id, diag_id, xhi_id]
    for n in (1, 2, 3):
        peers += [at(0, turn(zz, n), yy), at(0, zz, turn(yy, n))]
    for to in peers:
        pl.semaphore_signal(barrier, inc=1, device_id=to, device_id_type=MESH)

    loads = [
        pltpu.make_async_copy(res_h.at[0], nrm, ld_sem.at[0]),
        pltpu.make_async_copy(enc_h.at[0], enc_v, ld_sem.at[1]),
        pltpu.make_async_copy(gate_h.at[0], gate_v, ld_sem.at[2]),
        pltpu.make_async_copy(up_h.at[0], up_v, ld_sem.at[3]),
        pltpu.make_async_copy(down_h.at[0], down_v, ld_sem.at[4]),
        pltpu.make_async_copy(dec_h.at[0, 0], dec_v, ld_sem.at[5]),
    ]
    for load in loads:
        load.start()

    def loop(count, size, body):
        def run(i, _):
            body(pl.ds(pl.multiple_of(i * size, size), size))
            return 0

        lax.fori_loop(0, count // size, run, 0)

    loads[0].wait()

    def norm_rows(rows):
        x = nrm[rows, :].astype(F32)
        scale = lax.rsqrt(jnp.mean(x * x, axis=-1, keepdims=True) + 1e-6)
        nrm[rows, :] = (x * scale * gain_v[...]).astype(BF16)

    loop(T, 32, norm_rows)
    loads[1].wait()

    def enc_rows(rows):
        enc_b[rows, :] = enc_v[rows, :].astype(BF16)

    loop(W, 128, enc_rows)
    my_cols = pl.ds(pl.multiple_of(par * W, W), W)
    rows_copy = pltpu.make_async_copy(rows_t, rows_h, out_sem.at[2])

    pl.semaphore_wait(barrier, len(peers))
    pre_copy = []
    for c in range(2):
        rows = pl.ds(c * RT, RT)
        partial = jnp.dot(nrm[rows, my_cols], enc_b[...], preferred_element_type=F32)
        pos[rows, :] = partial
        pre_snd[rows, :] = partial.astype(BF16)
        pre_copy.append(remote(pre_snd.at[rows], pre_rcv.at[rows], pre_s.at[c], pre_r.at[c], par_id))
        pre_copy[c].start()

    loads[2].wait()
    loads[3].wait()

    def mlp_rows(rows):
        x = nrm[rows, :]
        g = lax.dot_general(x, gate_v[...], (((1,), (1,)), ((), ())), preferred_element_type=F32)
        u = lax.dot_general(x, up_v[...], (((1,), (1,)), ((), ())), preferred_element_type=F32)
        inner = 0.7978845608028654 * (g + 0.044715 * g * g * g)
        hid[rows, :] = (0.5 * g * (1.0 + jnp.tanh(inner)) * u).astype(BF16)

    loop(T, RT, mlp_rows)
    loads[4].wait()

    def role_of(u):
        return u if u < 2 else core

    def half_rows(blk, half):
        return pl.ds(pl.multiple_of(blk * Q1 + half * QH, QH), QH)

    def ring(u, m):
        role = role_of(u)
        i, k = first_of(role), second_of(role)
        up1, down1, far = turn(i, 1), turn(i, 3), turn(i, 2)
        right, left = at(role, up1, k), at(role, down1, k)
        src, to = [
            (lambda: part.at[u, half_rows(far, 0)], right),
            (lambda: part.at[u, half_rows(far, 1)], left),
            (lambda: part.at[u, half_rows(up1, 1)], right),
            (lambda: part.at[u, half_rows(down1, 0)], left),
            (lambda: relay.at[u, 0], right),
            (lambda: relay.at[u, 1], left),
        ][m]
        return remote(src(), r1_rcv.at[u, m], r1_s.at[u, m], r1_r.at[u, m], to)

    def ring_start(u):
        for m in range(4):
            ring(u, m).start()

    def ring_relay(u):
        i = first_of(role_of(u))
        for m, blk in ((0, turn(i, 1)), (1, turn(i, 3))):
            ring(u, m).wait_recv()
            relay[u, m] = (r1_rcv[u, m].astype(F32) + part[u, half_rows(blk, m), :].astype(F32)).astype(BF16)
            ring(u, 4 + m).start()

    def second_copy(u, n):
        role = role_of(u)
        to = at(role, first_of(role), turn(second_of(role), n))
        return remote(r2_snd.at[u, n - 1], r2_rcv.at[u, n - 1], r2_s.at[u, n - 1], r2_r.at[u, n - 1], to)

    def second_start(u):
        role = role_of(u)
        i, k = first_of(role), second_of(role)
        for m in (2, 3, 4, 5):
            ring(u, m).wait_recv()

        def piece(q):
            half = lax.div(q, 2)
            here = pl.ds(pl.multiple_of(lax.rem(q, 2) * Q2, Q2), Q2)
            rows = pl.ds(pl.multiple_of(i * Q1 + q * Q2, Q2), Q2)
            return (
                part[u, rows, :].astype(F32)
                + r1_rcv[u, 3 - half, here, :].astype(F32)
                + r1_rcv[u, 4 + half, here, :].astype(F32)
            )

        for n in (1, 2, 3):
            r2_snd[u, n - 1] = piece(turn(k, n)).astype(BF16)
            second_copy(u, n).start()
        fin[u] = piece(k)

    def second_end(u):
        for n in (1, 2, 3):
            second_copy(u, n).wait_recv()
        total = fin[u]
        for n in range(3):
            total = total + r2_rcv[u, n].astype(F32)
        fin[u] = total

    for h in range(2):

        def down_cols(local):
            cols = pl.ds(pl.multiple_of(local.start + h * W, CT), CT)
            part[h, :, local] = jnp.dot(hid[...], down_v[:, cols], preferred_element_type=F32).astype(BF16)

        loop(W, CT, down_cols)

        @pl.when(away)
        def _():
            ring_start(h)

    live0 = par >= layer
    live1 = 2 + par >= layer
    half_cols = pl.ds(pl.multiple_of(core * W, W), W)

    def activate(c):
        pre_copy[c].wait_recv()

        def act_rows(rows):
            rows = pl.ds(pl.multiple_of(c * RT + rows.start, 32), 32)
            p = jnp.maximum(pos[rows, :] + pre_rcv[rows, :].astype(F32) + ebias_v[...], 0.0)
            pos[rows, :] = p
            act[rows, :] = (p * p).astype(BF16)

        loop(RT, 32, act_rows)

    def core_copy(j, r):
        rows = pl.ds(r * RT, RT)
        return remote(cs_snd.at[j, rows], cs_rcv.at[j, rows], cs_s.at[j, r], cs_r.at[j, r], sib_id)

    def recon(j, r):
        live = (live1 if j == 1 else live0).astype(F32)
        ours = jnp.logical_and(home, x_hi == j).astype(F32)
        rows = pl.ds(r * RT, RT)
        x = act[rows, :]

        def tile(half, local):
            cols = pl.ds(pl.multiple_of(half * W + local.start, CT), CT)
            out = jnp.dot(x, dec_v[j, :, cols], preferred_element_type=F32)
            return out * live - part[half, rows, local].astype(F32) * ours

        def for_sibling(local):
            cs_snd[j, rows, local] = tile(1 - core, local).astype(BF16)

        def for_self(local):
            own[j, rows, local] = tile(core, local)

        loop(W, CT, for_sibling)
        core_copy(j, r).start()
        loop(W, CT, for_self)

    def chip_sum(j):
        for r in range(2):
            core_copy(j, r).wait_recv()

        def add_rows(rows):
            part[3 - j, rows, :] = (own[j, rows, :] + cs_rcv[j, rows, :].astype(F32)).astype(BF16)

        loop(T, 32, add_rows)

    tg_par = remote(tg_snd.at[0], tg_rcv, tg_s.at[0], tg_r, par_id)
    tg_diag = remote(tg_snd.at[1], tg_rcv, tg_s.at[1], tg_r, diag_id)

    activate(0)
    loads[5].wait()
    recon(1, 0)

    @pl.when(away)
    def _():
        ring_relay(0)
        ring_relay(1)

    activate(1)
    recon(1, 1)

    @pl.when(low)
    def _():
        recon(0, 0)

    chip_sum(1)
    ring_start(2)

    @pl.when(away)
    def _():
        second_start(0)
        second_start(1)

    @pl.when(low)
    def _():
        recon(0, 1)

    ring_relay(2)

    @pl.when(low)
    def _():
        chip_sum(0)
        ring_start(3)

    @pl.when(away)
    def _():
        second_end(0)
        second_end(1)
        tg_snd[0] = fin[core].astype(BF16)
        tg_snd[1] = fin[1 - core].astype(BF16)
        tg_par.start()
        tg_diag.start()

    second_start(2)

    @pl.when(low)
    def _():
        ring_relay(3)

    second_end(2)
    x_copy = remote(x_snd, x_rcv, x_s, x_r, xhi_id)
    a, b = first_of(core), second_of(core)
    my_rows = pl.ds(pl.multiple_of(a * Q1 + b * Q2, Q2), Q2)

    def write_error(j, total):
        bias = dbias_v[pl.ds(2 * j + par, 1), half_cols]
        err[core, j, my_rows, :] = ((total + bias) * 0.0625).astype(BF16)

    def take_target(u):
        tg_par.wait_recv()
        fin[u] = fin[u] - tg_rcv[...].astype(F32)

    @pl.when(jnp.logical_not(low))
    def _():
        take_target(2)

    x_snd[...] = fin[2].astype(BF16)
    x_copy.start()
    act_t[...] = act[...].T
    for n in range(W // CT):
        cols = pl.ds(pl.multiple_of(par * W + n * CT, 128), CT)
        rows_t[pl.ds(n * CT, CT), :] = nrm[:, cols].T
    rows_copy.start()

    @pl.when(low)
    def _():
        second_start(3)

    def block(first):
        return pl.ds(pl.multiple_of(first * Q1, Q1), Q1)

    def gather_a(j, n):
        piece = err.at[core, j, my_rows]
        return remote(piece, piece, ga_s.at[j, n - 1], ga_r.at[j, n - 1], at(core, a, turn(b, n)))

    def gather_b(j, m):
        rows, n = [
            (block(a), 1), (block(a), 3), (half_rows(turn(a, 3), 0), 1), (half_rows(turn(a, 1), 1), 3)
        ][m]
        piece = err.at[core, j, rows]
        return remote(piece, piece, gb_s.at[j, m], gb_r.at[j, m], at(core, turn(a, n), b))

    def gather_c(j, n):
        piece = err.at[core, j, block(turn(a, n))]
        return remote(piece, piece, gc_s.at[j, n], gc_r.at[j, n], sib_id)

    def gather_1(j):
        for n in (1, 2, 3):
            gather_a(j, n).start()

    def gather_2(j):
        for n in (1, 2, 3):
            gather_a(j, n).wait_recv()
        gather_b(j, 0).start()
        gather_b(j, 1).start()
        gather_c(j, 0).start()

    def gather_3(j):
        gather_b(j, 0).wait_recv()
        gather_b(j, 2).start()
        gather_c(j, 3).start()
        gather_b(j, 1).wait_recv()
        gather_b(j, 3).start()
        gather_c(j, 1).start()

    def gather_4(j):
        gather_b(j, 2).wait_recv()
        gather_b(j, 3).wait_recv()
        gather_c(j, 2).start()

    def wait_error(j):
        for n in range(4):
            gather_c(j, n).wait_recv()

    def back_tile(j, rows):
        out = None
        for h in range(2):
            term = lax.dot_general(
                err[h, j, rows, :], dec_v[j, :, pl.ds(h * W, W)], (((1,), (1,)), ((), ())),
                preferred_element_type=F32,
            )
            out = term if out is None else out + term
        return out

    def dec_grad(j):
        for h in range(2):

            def grad_cols(local):
                cols = pl.ds(pl.multiple_of(local.start + h * W, CT), CT)
                dg_v[j, :, cols] = jnp.dot(
                    act_t[...], err[h, j, :, local], preferred_element_type=F32
                ).astype(BF16)

            loop(W, CT, grad_cols)

    def no_dec_grad(j):
        def zero_rows(rows):
            dg_v[j, rows, :] = jnp.zeros((32, D), BF16)

        loop(F, 32, zero_rows)

    outs = [pltpu.make_async_copy(dg_v.at[j], dgrad_h.at[j], out_sem.at[j]) for j in range(2)]

    x_copy.wait_recv()
    write_error(1, fin[2] + x_rcv[...].astype(F32))
    gather_1(1)

    @pl.when(low)
    def _():
        second_end(3)
        take_target(3)
        write_error(0, fin[3])
        gather_1(0)

    gather_2(1)

    @pl.when(low)
    def _():
        gather_2(0)

    gather_3(1)

    @pl.when(low)
    def _():
        gather_3(0)

    gather_4(1)
    wait_error(1)

    def back_first(r):
        rows = pl.ds(r * RT, RT)

        @pl.when(live1)
        def _():
            back[rows, :] = back_tile(1, rows)

        @pl.when(jnp.logical_not(live1))
        def _():
            back[rows, :] = jnp.zeros((RT, F), F32)

    back_first(0)

    @pl.when(low)
    def _():
        gather_4(0)

    back_first(1)

    @pl.when(low)
    def _():
        wait_error(0)

    bk_copy = []
    for r in range(T // BT):
        rows = pl.ds(r * BT, BT)

        @pl.when(live0)
        def _():
            back[rows, :] += back_tile(0, rows)

        bk_snd[rows, :] = back[rows, :].astype(BF16)
        bk_copy.append(remote(bk_snd.at[rows], bk_rcv.at[rows], bk_s.at[r], bk_r.at[r], par_id))
        bk_copy[r].start()

    for j, live in ((1, live1), (0, live0)):

        @pl.when(live)
        def _():
            dec_grad(j)

        @pl.when(jnp.logical_not(live))
        def _():
            no_dec_grad(j)

        outs[j].start()

    bgrad_v[...] = jnp.zeros((1, F), F32)
    for r in range(T // BT):
        bk_copy[r].wait_recv()

        def dpre_rows(rows):
            rows = pl.ds(pl.multiple_of(r * BT + rows.start, 32), 32)
            d = (back[rows, :] + bk_rcv[rows, :].astype(F32)) * 2.0 * pos[rows, :]
            dpre[rows, :] = d.astype(BF16)
            bgrad_v[...] += jnp.sum(d, axis=0, keepdims=True)

        loop(BT, 32, dpre_rows)

    last = pltpu.make_async_copy(dpre, dpre_h, out_sem.at[3])
    last.start()

    for copy in pre_copy + bk_copy:
        copy.wait_send()

    def drain(u, j):
        for m in range(6):
            ring(u, m).wait_send()
        for n in (1, 2, 3):
            second_copy(u, n).wait_send()
        if j is not None:
            for r in range(2):
                core_copy(j, r).wait_send()
            for n in (1, 2, 3):
                gather_a(j, n).wait_send()
            for n in range(4):
                gather_b(j, n).wait_send()
                gather_c(j, n).wait_send()

    drain(2, 1)

    @pl.when(low)
    def _():
        drain(3, 0)

    @pl.when(away)
    def _():
        drain(0, None)
        drain(1, None)
        tg_par.wait_send()
        tg_diag.wait_send()

    x_copy.wait_send()
    for copy in outs:
        copy.wait()
    rows_copy.wait()
    last.wait()


def finish_kernel(
    rows_h, dpre_h, bsum_v, dgrad_h, egrad_h, bgrad_v, dout_h, rows_v, dpre_v, eg_v, dg_v, ld_sem, in_sem, out_sem, cp_sem
):
    loads = [
        pltpu.make_async_copy(dpre_h, dpre_v, ld_sem.at[0]),
        pltpu.make_async_copy(rows_h, rows_v, ld_sem.at[1]),
    ]
    here = [(j, pl.ds(r * RT, RT)) for j in range(2) for r in range(2)]
    arrive = [pltpu.make_async_copy(dgrad_h.at[p], dg_v.at[p], in_sem.at[n]) for n, p in enumerate(here)]
    leave = [pltpu.make_async_copy(dg_v.at[p], dout_h.at[(0, 0) + p], cp_sem.at[n]) for n, p in enumerate(here)]
    for copy in loads + arrive:
        copy.start()
    for copy in loads:
        copy.wait()
    bgrad_v[...] = bsum_v[...]
    outs = []
    for n in range(W // CT):
        rows = pl.ds(n * CT, CT)
        eg_v[rows, :] = jnp.dot(rows_v[rows, :], dpre_v[...], preferred_element_type=F32)
        outs.append(pltpu.make_async_copy(eg_v.at[rows], egrad_h.at[0, rows], out_sem.at[n]))
        outs[n].start()
        arrive[n].wait()
        leave[n].start()
    arrive[3].wait()
    leave[3].start()
    for copy in outs + leave:
        copy.wait()


def shards(
    residual, norm_gain, gate_weight, up_weight, down_weight, enc_weight, enc_bias, dec_weight, dec_bias
):
    any_spec = pl.BlockSpec(memory_space=pl.ANY)
    vmem = pl.BlockSpec(memory_space=pltpu.VMEM)
    dma = pltpu.SemaphoreType.DMA

    def pair(*shape):
        return [dma(shape), dma(shape)]

    scratch = [
        pltpu.VMEM((T, D), BF16),
        pltpu.VMEM((W, T), BF16),
        pltpu.VMEM((U, D), BF16),
        pltpu.VMEM((U, D), BF16),
        pltpu.VMEM((U, D), BF16),
        pltpu.VMEM((T, U), BF16),
        pltpu.VMEM((W, F), F32),
        pltpu.VMEM((W, F), BF16),
        pltpu.VMEM((2, F, D), BF16),
        pltpu.VMEM((T, F), BF16),
        pltpu.VMEM((T, F), BF16),
        pltpu.VMEM((T, F), F32),
        pltpu.VMEM((T, F), BF16),
        pltpu.VMEM((F, T), BF16),
        pltpu.VMEM((2, T, W), F32),
        pltpu.VMEM((2, T, W), BF16),
        pltpu.VMEM((2, T, W), BF16),
        pltpu.VMEM((4, T, W), BF16),
        pltpu.VMEM((4, 2, QH, W), BF16),
        pltpu.VMEM((4, 6, QH, W), BF16),
        pltpu.VMEM((4, 3, Q2, W), BF16),
        pltpu.VMEM((4, 3, Q2, W), BF16),
        pltpu.VMEM((4, Q2, W), F32),
        pltpu.VMEM((2, Q2, W), BF16),
        pltpu.VMEM((Q2, W), BF16),
        pltpu.VMEM((Q2, W), BF16),
        pltpu.VMEM((Q2, W), BF16),
        pltpu.VMEM((2, 2, T, W), BF16),
        pltpu.VMEM((T, F), F32),
        pltpu.VMEM((T, F), BF16),
        pltpu.VMEM((T, F), BF16),
        pltpu.VMEM((T, F), BF16),
        pltpu.VMEM((2, F, D), BF16),
        dma((6,)), dma((4,)),
    ]
    scratch += pair(2) + pair(2, 2) + pair(4, 6) + pair(4, 3)
    scratch += [dma((2,)), dma, dma, dma]
    scratch += pair(2, 3) + pair(2, 4) + pair(2, 4) + pair(T // BT)
    rows, dpre, bsum, dgrad = pl.pallas_call(
        kernel,
        out_shape=(
            jax.ShapeDtypeStruct((W, T), BF16),
            jax.ShapeDtypeStruct((T, F), BF16),
            jax.ShapeDtypeStruct((1, F), F32),
            jax.ShapeDtypeStruct((2, F, D), BF16),
        ),
        in_specs=[any_spec, vmem, any_spec, any_spec, any_spec, any_spec, vmem, any_spec, vmem],
        out_specs=(any_spec, any_spec, vmem, any_spec),
        scratch_shapes=scratch,
        compiler_params=pltpu.CompilerParams(
            collective_id=0, has_side_effects=True, vmem_limit_bytes=62 * 1024 * 1024
        ),
    )(
        residual,
        norm_gain,
        jnp.swapaxes(gate_weight, 1, 2),
        jnp.swapaxes(up_weight, 1, 2),
        down_weight,
        enc_weight,
        enc_bias,
        dec_weight,
        dec_bias,
    )
    return pl.pallas_call(
        finish_kernel,
        out_shape=(
            jax.ShapeDtypeStruct((1, W, F), F32),
            jax.ShapeDtypeStruct((1, F), F32),
            jax.ShapeDtypeStruct((1, 1, 2, F, D), BF16),
        ),
        in_specs=[any_spec, any_spec, vmem, any_spec],
        out_specs=(any_spec, vmem, any_spec),
        scratch_shapes=[
            pltpu.VMEM((W, T), BF16),
            pltpu.VMEM((T, F), BF16),
            pltpu.VMEM((W, F), F32),
            pltpu.VMEM((2, F, D), BF16),
            dma((2,)),
            dma((4,)),
            dma((W // CT,)),
            dma((4,)),
        ],
        compiler_params=pltpu.CompilerParams(vmem_limit_bytes=62 * 1024 * 1024),
    )(rows, dpre, bsum, dgrad)


def solution(mesh):
    return jax.shard_map(
        shards,
        mesh=mesh,
        in_specs=(
            P("layer", None, None),
            P("layer", None),
            P("layer", None, ("feat", "par")),
            P("layer", None, ("feat", "par")),
            P("layer", ("feat", "par"), None),
            P("layer", "par", "feat"),
            P("layer", "feat"),
            P("layer", "par", None, "feat", None),
            P(),
        ),
        out_specs=(
            P("layer", "par", "feat"),
            P("layer", "feat"),
            P("layer", "par", None, "feat", None),
        ),
        check_vma=False,
    )
```

```python
import jax
import jax.numpy as jnp
from jax import lax
from jax.experimental import pallas as pl
from jax.experimental.pallas import tpu as pltpu
from jax.sharding import PartitionSpec as P

F32 = jnp.float32
BF16 = jnp.bfloat16
MESH = pl.DeviceIdType.MESH

T = 512
D = 2304
W = D // 2
F = 512
U = 288
RT = 256
Q1 = RT // 4
QH = Q1 // 2
Q2 = RT // 16
CT = 384
BT = 128


def kernel(
    res_h, gain_v, gate_h, up_h, down_h, enc_h, ebias_v, dec_h, dbias_v,
    rows_h, dpre_h, bgrad_v, dgrad_h,
    nrm, rows_t, gate_v, up_v, down_v, hid, enc_v, enc_b, dec_v,
    pre_snd, pre_rcv, pos, act, act_t,
    own, cs_snd, cs_rcv, part, relay, r1_rcv, r2_snd, r2_rcv, fin, tg_snd, tg_rcv, x_snd, x_rcv,
    err, back, bk_snd, bk_rcv, dpre, dg_v,
    ld_sem, out_sem, pre_s, pre_r, cs_s, cs_r, r1_s, r1_r, r2_s, r2_r, tg_s, tg_r, x_s, x_r,
    ga_s, ga_r, gb_s, gb_r, gc_s, gc_r, bk_s, bk_r,
):
    layer = lax.axis_index("layer")
    feat = lax.axis_index("feat")
    par = lax.axis_index("par")
    core = lax.rem(layer, 2)
    x_hi = lax.div(layer, 2)
    zz = lax.div(feat, 4)
    yy = lax.rem(feat, 4)
    low = x_hi == 0
    home = core == par
    away = core != par

    def first_of(role):
        return zz + role * (yy - zz)

    def second_of(role):
        return yy + role * (zz - yy)

    def at(role, first, second):
        return (layer, first * 4 + second + role * 3 * (second - first), par)

    def turn(x, n):
        return lax.rem(x + n, 4)

    sib = layer + 1 - 2 * core
    par_id = (layer, feat, 1 - par)
    sib_id = (sib, feat, par)
    diag_id = (sib, feat, 1 - par)
    xhi_id = (turn(layer, 2), feat, par)

    def remote(src, dst, s, r, to):
        return pltpu.make_async_remote_copy(
            src_ref=src, dst_ref=dst, send_sem=s, recv_sem=r, device_id=to, device_id_type=MESH
        )

    barrier = pltpu.get_barrier_semaphore()
    peers = [par_id, sib_id, diag_id, xhi_id]
    for n in (1, 2, 3):
        peers += [at(0, turn(zz, n), yy), at(0, zz, turn(yy, n))]
    for to in peers:
        pl.semaphore_signal(barrier, inc=1, device_id=to, device_id_type=MESH)

    loads = [
        pltpu.make_async_copy(res_h.at[0], nrm, ld_sem.at[0]),
        pltpu.make_async_copy(enc_h.at[0], enc_v, ld_sem.at[1]),
        pltpu.make_async_copy(gate_h.at[0], gate_v, ld_sem.at[2]),
        pltpu.make_async_copy(up_h.at[0], up_v, ld_sem.at[3]),
        pltpu.make_async_copy(down_h.at[0], down_v, ld_sem.at[4]),
        pltpu.make_async_copy(dec_h.at[0, 0], dec_v, ld_sem.at[5]),
    ]
    for load in loads:
        load.start()

    def loop(count, size, body):
        def run(i, _):
            body(pl.ds(pl.multiple_of(i * size, size), size))
            return 0

        lax.fori_loop(0, count // size, run, 0)

    loads[0].wait()

    def norm_rows(rows):
        x = nrm[rows, :].astype(F32)
        scale = lax.rsqrt(jnp.mean(x * x, axis=-1, keepdims=True) + 1e-6)
        nrm[rows, :] = (x * scale * gain_v[...]).astype(BF16)

    loop(T, 32, norm_rows)
    loads[1].wait()

    def enc_rows(rows):
        enc_b[rows, :] = enc_v[rows, :].astype(BF16)

    loop(W, 128, enc_rows)
    my_cols = pl.ds(pl.multiple_of(par * W, W), W)
    rows_copy = pltpu.make_async_copy(rows_t, rows_h, out_sem.at[2])

    pl.semaphore_wait(barrier, len(peers))
    pre_copy = []
    for c in range(2):
        rows = pl.ds(c * RT, RT)
        partial = jnp.dot(nrm[rows, my_cols], enc_b[...], preferred_element_type=F32)
        pos[rows, :] = partial
        pre_snd[rows, :] = partial.astype(BF16)
        pre_copy.append(remote(pre_snd.at[rows], pre_rcv.at[rows], pre_s.at[c], pre_r.at[c], par_id))
        pre_copy[c].start()

    loads[2].wait()
    loads[3].wait()

    def mlp_rows(rows):
        x = nrm[rows, :]
        g = lax.dot_general(x, gate_v[...], (((1,), (1,)), ((), ())), preferred_element_type=F32)
        u = lax.dot_general(x, up_v[...], (((1,), (1,)), ((), ())), preferred_element_type=F32)
        inner = 0.7978845608028654 * (g + 0.044715 * g * g * g)
        hid[rows, :] = (0.5 * g * (1.0 + jnp.tanh(inner)) * u).astype(BF16)

    def mlp(t):
        mlp_rows(pl.ds(t * RT, RT))
        for h in range(2):

            def down_cols(local):
                cols = pl.ds(pl.multiple_of(local.start + h * W, CT), CT)
                part[2 * t + h, :, local] = jnp.dot(
                    hid[t * RT : (t + 1) * RT, :], down_v[:, cols], preferred_element_type=F32
                ).astype(BF16)

            loop(W, CT, down_cols)

            @pl.when(away)
            def _():
                ring_start(2 * t + h)

    def role_of(u):
        return u % 2 if u < 4 else core

    def half_rows(blk, half):
        return pl.ds(pl.multiple_of(blk * Q1 + half * QH, QH), QH)

    def ring(u, m):
        role = role_of(u)
        i, k = first_of(role), second_of(role)
        up1, down1, far = turn(i, 1), turn(i, 3), turn(i, 2)
        right, left = at(role, up1, k), at(role, down1, k)
        src, to = [
            (lambda: part.at[u, half_rows(far, 0)], right),
            (lambda: part.at[u, half_rows(far, 1)], left),
            (lambda: part.at[u, half_rows(up1, 1)], right),
            (lambda: part.at[u, half_rows(down1, 0)], left),
            (lambda: relay.at[u, 0], right),
            (lambda: relay.at[u, 1], left),
        ][m]
        return remote(src(), r1_rcv.at[u, m], r1_s.at[u, m], r1_r.at[u, m], to)

    def ring_start(u):
        for m in range(4):
            ring(u, m).start()

    def ring_relay(u):
        i = first_of(role_of(u))
        for m, blk in ((0, turn(i, 1)), (1, turn(i, 3))):
            ring(u, m).wait_recv()
            relay[u, m] = (r1_rcv[u, m].astype(F32) + part[u, half_rows(blk, m), :].astype(F32)).astype(BF16)
            ring(u, 4 + m).start()

    def second_copy(u, n):
        role = role_of(u)
        to = at(role, first_of(role), turn(second_of(role), n))
        return remote(r2_snd.at[u, n - 1], r2_rcv.at[u, n - 1], r2_s.at[u, n - 1], r2_r.at[u, n - 1], to)

    def second_start(u):
        role = role_of(u)
        i, k = first_of(role), second_of(role)
        for m in (2, 3, 4, 5):
            ring(u, m).wait_recv()

        def piece(q):
            half = lax.div(q, 2)
            here = pl.ds(pl.multiple_of(lax.rem(q, 2) * Q2, Q2), Q2)
            rows = pl.ds(pl.multiple_of(i * Q1 + q * Q2, Q2), Q2)
            return (
                part[u, rows, :].astype(F32)
                + r1_rcv[u, 3 - half, here, :].astype(F32)
                + r1_rcv[u, 4 + half, here, :].astype(F32)
            )

        for n in (1, 2, 3):
            r2_snd[u, n - 1] = piece(turn(k, n)).astype(BF16)
            second_copy(u, n).start()
        fin[u] = piece(k)

    def second_end(u):
        for n in (1, 2, 3):
            second_copy(u, n).wait_recv()
        total = fin[u]
        for n in range(3):
            total = total + r2_rcv[u, n].astype(F32)
        fin[u] = total

    live0 = par >= layer
    live1 = 2 + par >= layer
    half_cols = pl.ds(pl.multiple_of(core * W, W), W)

    def activate(c):
        pre_copy[c].wait_recv()

        def act_rows(rows):
            rows = pl.ds(pl.multiple_of(c * RT + rows.start, 32), 32)
            p = jnp.maximum(pos[rows, :] + pre_rcv[rows, :].astype(F32) + ebias_v[...], 0.0)
            pos[rows, :] = p
            act[rows, :] = (p * p).astype(BF16)

        loop(RT, 32, act_rows)

    def core_copy(j, r):
        rows = pl.ds(r * RT, RT)
        return remote(cs_snd.at[j, rows], cs_rcv.at[j, rows], cs_s.at[j, r], cs_r.at[j, r], sib_id)

    def recon(j, r):
        live = (live1 if j == 1 else live0).astype(F32)
        ours = jnp.logical_and(home, x_hi == j).astype(F32)
        rows = pl.ds(r * RT, RT)
        x = act[rows, :]

        def tile(half, local):
            cols = pl.ds(pl.multiple_of(half * W + local.start, CT), CT)
            out = jnp.dot(x, dec_v[j, :, cols], preferred_element_type=F32)
            return out * live - part[2 * r + half, :, local].astype(F32) * ours

        def for_sibling(local):
            cs_snd[j, rows, local] = tile(1 - core, local).astype(BF16)

        def for_self(local):
            own[j, rows, local] = tile(core, local)

        loop(W, CT, for_sibling)
        core_copy(j, r).start()
        loop(W, CT, for_self)

    def chip_sum(j, t):
        core_copy(j, t).wait_recv()

        def add_rows(rows):
            whole = pl.ds(pl.multiple_of(t * RT + rows.start, 32), 32)
            part[unit(j, t), rows, :] = (own[j, whole, :] + cs_rcv[j, whole, :].astype(F32)).astype(BF16)

        loop(RT, 32, add_rows)
        ring_start(unit(j, t))

    def unit(j, t):
        return 5 + 2 * t - j

    def tg_par(t):
        return remote(tg_snd.at[t, 0], tg_rcv.at[t], tg_s.at[t, 0], tg_r.at[t], par_id)

    def tg_diag(t):
        return remote(tg_snd.at[t, 1], tg_rcv.at[t], tg_s.at[t, 1], tg_r.at[t], diag_id)

    def x_copy(t):
        return remote(x_snd.at[t], x_rcv.at[t], x_s.at[t], x_r.at[t], xhi_id)

    a, b = first_of(core), second_of(core)

    def piece_rows(t):
        return pl.ds(pl.multiple_of(t * RT + a * Q1 + b * Q2, Q2), Q2)

    def write_error(j, t, total):
        bias = dbias_v[pl.ds(2 * j + par, 1), half_cols]
        err[core, j, piece_rows(t), :] = ((total + bias) * 0.0625).astype(BF16)

    def take_target(j, t):
        tg_par(t).wait_recv()
        fin[unit(j, t)] = fin[unit(j, t)] - tg_rcv[t].astype(F32)

    def block(t, first):
        return pl.ds(pl.multiple_of(t * RT + first * Q1, Q1), Q1)

    def half_block(t, first, half):
        return pl.ds(pl.multiple_of(t * RT + first * Q1 + half * QH, QH), QH)

    def gather_a(j, t, n):
        piece = err.at[core, j, piece_rows(t)]
        return remote(piece, piece, ga_s.at[2 * j + t, n - 1], ga_r.at[2 * j + t, n - 1], at(core, a, turn(b, n)))

    def gather_b(j, t, m):
        rows, n = [
            (block(t, a), 1),
            (block(t, a), 3),
            (half_block(t, turn(a, 3), 0), 1),
            (half_block(t, turn(a, 1), 1), 3),
        ][m]
        piece = err.at[core, j, rows]
        return remote(piece, piece, gb_s.at[2 * j + t, m], gb_r.at[2 * j + t, m], at(core, turn(a, n), b))

    def gather_c(j, t, n):
        piece = err.at[core, j, block(t, turn(a, n))]
        return remote(piece, piece, gc_s.at[2 * j + t, n], gc_r.at[2 * j + t, n], sib_id)

    def gather_1(j, t):
        for n in (2, 1, 3):
            gather_a(j, t, n).start()

    def gather_2(j, t):
        for n in (1, 3, 2):
            gather_a(j, t, n).wait_recv()
        gather_b(j, t, 0).start()
        gather_b(j, t, 1).start()
        gather_c(j, t, 0).start()

    def gather_3(j, t):
        gather_b(j, t, 0).wait_recv()
        gather_b(j, t, 2).start()
        gather_c(j, t, 3).start()
        gather_b(j, t, 1).wait_recv()
        gather_b(j, t, 3).start()
        gather_c(j, t, 1).start()

    def gather_4(j, t):
        gather_b(j, t, 2).wait_recv()
        gather_b(j, t, 3).wait_recv()
        gather_c(j, t, 2).start()

    def wait_error(j, t):
        for n in (0, 1, 3, 2):
            gather_c(j, t, n).wait_recv()

    def each(stage, t):
        stage(1, t)

        @pl.when(low)
        def _():
            stage(0, t)

    def target(stage, t):
        @pl.when(away)
        def _():
            for h in range(2):
                stage(2 * t + h)

    def send_target(t):
        @pl.when(away)
        def _():
            second_end(2 * t)
            second_end(2 * t + 1)
            tg_snd[t, 0] = fin[2 * t + core].astype(BF16)
            tg_snd[t, 1] = fin[2 * t + 1 - core].astype(BF16)
            tg_par(t).start()
            tg_diag(t).start()

    def send_slot_1(t):
        second_end(unit(1, t))

        @pl.when(jnp.logical_not(low))
        def _():
            take_target(1, t)

        x_snd[t] = fin[unit(1, t)].astype(BF16)
        x_copy(t).start()

    def error_1(t):
        x_copy(t).wait_recv()
        write_error(1, t, fin[unit(1, t)] + x_rcv[t].astype(F32))
        gather_1(1, t)

    def error_0(t):
        @pl.when(low)
        def _():
            second_end(unit(0, t))
            take_target(0, t)
            write_error(0, t, fin[unit(0, t)])
            gather_1(0, t)

    def relay_of(j, t):
        ring_relay(unit(j, t))

    def second_of_unit(j, t):
        second_start(unit(j, t))

    loads[4].wait()
    mlp(0)
    activate(0)
    loads[5].wait()
    each(recon, 0)
    target(ring_relay, 0)
    each(chip_sum, 0)
    mlp(1)
    target(second_start, 0)
    each(relay_of, 0)
    activate(1)
    each(recon, 1)
    each(second_of_unit, 0)
    target(ring_relay, 1)
    send_target(0)
    each(chip_sum, 1)
    send_slot_1(0)
    error_0(0)
    target(second_start, 1)
    each(relay_of, 1)
    error_1(0)

    act_t[...] = act[...].T
    for n in range(W // CT):
        cols = pl.ds(pl.multiple_of(par * W + n * CT, 128), CT)
        rows_t[pl.ds(n * CT, CT), :] = nrm[:, cols].T
    rows_copy.start()

    each(second_of_unit, 1)
    send_target(1)
    each(gather_2, 0)
    send_slot_1(1)
    error_0(1)
    error_1(1)
    each(gather_3, 0)
    each(gather_2, 1)
    each(gather_4, 0)
    each(wait_error, 0)

    def back_tile(j, rows):
        out = None
        for h in range(2):
            term = lax.dot_general(
                err[h, j, rows, :], dec_v[j, :, pl.ds(h * W, W)], (((1,), (1,)), ((), ())),
                preferred_element_type=F32,
            )
            out = term if out is None else out + term
        return out

    def dec_grad(j):
        for h in range(2):

            def grad_cols(local):
                cols = pl.ds(pl.multiple_of(local.start + h * W, CT), CT)
                dg_v[j, :, cols] = jnp.dot(
                    act_t[...], err[h, j, :, local], preferred_element_type=F32
                ).astype(BF16)

            loop(W, CT, grad_cols)

    def no_dec_grad(j):
        def zero_rows(rows):
            dg_v[j, rows, :] = jnp.zeros((32, D), BF16)

        loop(F, 32, zero_rows)

    outs = [pltpu.make_async_copy(dg_v.at[j], dgrad_h.at[j], out_sem.at[j]) for j in range(2)]

    bk_copy = []

    def back_rows(r):
        rows = pl.ds(r * BT, BT)

        @pl.when(live1)
        def _():
            back[rows, :] = back_tile(1, rows)

        @pl.when(jnp.logical_not(live1))
        def _():
            back[rows, :] = jnp.zeros((BT, F), F32)

        @pl.when(live0)
        def _():
            back[rows, :] += back_tile(0, rows)

        bk_snd[rows, :] = back[rows, :].astype(BF16)
        bk_copy.append(remote(bk_snd.at[rows], bk_rcv.at[rows], bk_s.at[r], bk_r.at[r], par_id))
        bk_copy[r].start()

    each(gather_3, 1)
    for r in range(T // BT // 2):
        back_rows(r)
    each(gather_4, 1)
    each(wait_error, 1)
    for r in range(T // BT // 2, T // BT):
        back_rows(r)

    for j, live in ((1, live1), (0, live0)):

        @pl.when(live)
        def _():
            dec_grad(j)

        @pl.when(jnp.logical_not(live))
        def _():
            no_dec_grad(j)

        outs[j].start()

    bgrad_v[...] = jnp.zeros((1, F), F32)
    for r in range(T // BT):
        bk_copy[r].wait_recv()

        def dpre_rows(rows):
            rows = pl.ds(pl.multiple_of(r * BT + rows.start, 32), 32)
            d = (back[rows, :] + bk_rcv[rows, :].astype(F32)) * 2.0 * pos[rows, :]
            dpre[rows, :] = d.astype(BF16)
            bgrad_v[...] += jnp.sum(d, axis=0, keepdims=True)

        loop(BT, 32, dpre_rows)

    last = pltpu.make_async_copy(dpre, dpre_h, out_sem.at[3])
    last.start()

    for copy in pre_copy + bk_copy:
        copy.wait_send()

    def drain(u):
        for m in range(6):
            ring(u, m).wait_send()
        for n in (1, 2, 3):
            second_copy(u, n).wait_send()

    def drain_slot(j, t):
        drain(unit(j, t))
        core_copy(j, t).wait_send()
        for n in (1, 2, 3):
            gather_a(j, t, n).wait_send()
        for n in range(4):
            gather_b(j, t, n).wait_send()
            gather_c(j, t, n).wait_send()

    for t in range(2):
        each(drain_slot, t)
        target(drain, t)
        x_copy(t).wait_send()

    @pl.when(away)
    def _():
        for t in range(2):
            tg_par(t).wait_send()
            tg_diag(t).wait_send()

    for copy in outs:
        copy.wait()
    rows_copy.wait()
    last.wait()


def finish_kernel(
    rows_h, dpre_h, bsum_v, dgrad_h, egrad_h, bgrad_v, dout_h, rows_v, dpre_v, eg_v, dg_v, ld_sem, in_sem, out_sem, cp_sem
):
    loads = [
        pltpu.make_async_copy(dpre_h, dpre_v, ld_sem.at[0]),
        pltpu.make_async_copy(rows_h, rows_v, ld_sem.at[1]),
    ]
    here = [(j, pl.ds(r * RT, RT)) for j in range(2) for r in range(2)]
    arrive = [pltpu.make_async_copy(dgrad_h.at[p], dg_v.at[p], in_sem.at[n]) for n, p in enumerate(here)]
    leave = [pltpu.make_async_copy(dg_v.at[p], dout_h.at[(0, 0) + p], cp_sem.at[n]) for n, p in enumerate(here)]
    for copy in loads + arrive:
        copy.start()
    for copy in loads:
        copy.wait()
    bgrad_v[...] = bsum_v[...]
    outs = []
    for n in range(W // CT):
        rows = pl.ds(n * CT, CT)
        eg_v[rows, :] = jnp.dot(rows_v[rows, :], dpre_v[...], preferred_element_type=F32)
        outs.append(pltpu.make_async_copy(eg_v.at[rows], egrad_h.at[0, rows], out_sem.at[n]))
        outs[n].start()
        arrive[n].wait()
        leave[n].start()
    arrive[3].wait()
    leave[3].start()
    for copy in outs + leave:
        copy.wait()


def shards(
    residual, norm_gain, gate_weight, up_weight, down_weight, enc_weight, enc_bias, dec_weight, dec_bias
):
    any_spec = pl.BlockSpec(memory_space=pl.ANY)
    vmem = pl.BlockSpec(memory_space=pltpu.VMEM)
    dma = pltpu.SemaphoreType.DMA

    def pair(*shape):
        return [dma(shape), dma(shape)]

    scratch = [
        pltpu.VMEM((T, D), BF16),
        pltpu.VMEM((W, T), BF16),
        pltpu.VMEM((U, D), BF16),
        pltpu.VMEM((U, D), BF16),
        pltpu.VMEM((U, D), BF16),
        pltpu.VMEM((T, U), BF16),
        pltpu.VMEM((W, F), F32),
        pltpu.VMEM((W, F), BF16),
        pltpu.VMEM((2, F, D), BF16),
        pltpu.VMEM((T, F), BF16),
        pltpu.VMEM((T, F), BF16),
        pltpu.VMEM((T, F), F32),
        pltpu.VMEM((T, F), BF16),
        pltpu.VMEM((F, T), BF16),
        pltpu.VMEM((2, T, W), F32),
        pltpu.VMEM((2, T, W), BF16),
        pltpu.VMEM((2, T, W), BF16),
        pltpu.VMEM((8, RT, W), BF16),
        pltpu.VMEM((8, 2, QH, W), BF16),
        pltpu.VMEM((8, 6, QH, W), BF16),
        pltpu.VMEM((8, 3, Q2, W), BF16),
        pltpu.VMEM((8, 3, Q2, W), BF16),
        pltpu.VMEM((8, Q2, W), F32),
        pltpu.VMEM((2, 2, Q2, W), BF16),
        pltpu.VMEM((2, Q2, W), BF16),
        pltpu.VMEM((2, Q2, W), BF16),
        pltpu.VMEM((2, Q2, W), BF16),
        pltpu.VMEM((2, 2, T, W), BF16),
        pltpu.VMEM((T, F), F32),
        pltpu.VMEM((T, F), BF16),
        pltpu.VMEM((T, F), BF16),
        pltpu.VMEM((T, F), BF16),
        pltpu.VMEM((2, F, D), BF16),
        dma((6,)), dma((4,)),
    ]
    scratch += pair(2) + pair(2, 2) + pair(8, 6) + pair(8, 3)
    scratch += [dma((2, 2)), dma((2,))] + pair(2)
    scratch += pair(4, 3) + pair(4, 4) + pair(4, 4) + pair(T // BT)
    rows, dpre, bsum, dgrad = pl.pallas_call(
        kernel,
        out_shape=(
            jax.ShapeDtypeStruct((W, T), BF16),
            jax.ShapeDtypeStruct((T, F), BF16),
            jax.ShapeDtypeStruct((1, F), F32),
            jax.ShapeDtypeStruct((2, F, D), BF16),
        ),
        in_specs=[any_spec, vmem, any_spec, any_spec, any_spec, any_spec, vmem, any_spec, vmem],
        out_specs=(any_spec, any_spec, vmem, any_spec),
        scratch_shapes=scratch,
        compiler_params=pltpu.CompilerParams(
            collective_id=0, has_side_effects=True, vmem_limit_bytes=62 * 1024 * 1024
        ),
    )(
        residual,
        norm_gain,
        jnp.swapaxes(gate_weight, 1, 2),
        jnp.swapaxes(up_weight, 1, 2),
        down_weight,
        enc_weight,
        enc_bias,
        dec_weight,
        dec_bias,
    )
    return pl.pallas_call(
        finish_kernel,
        out_shape=(
            jax.ShapeDtypeStruct((1, W, F), F32),
            jax.ShapeDtypeStruct((1, F), F32),
            jax.ShapeDtypeStruct((1, 1, 2, F, D), BF16),
        ),
        in_specs=[any_spec, any_spec, vmem, any_spec],
        out_specs=(any_spec, vmem, any_spec),
        scratch_shapes=[
            pltpu.VMEM((W, T), BF16),
            pltpu.VMEM((T, F), BF16),
            pltpu.VMEM((W, F), F32),
            pltpu.VMEM((2, F, D), BF16),
            dma((2,)),
            dma((4,)),
            dma((W // CT,)),
            dma((4,)),
        ],
        compiler_params=pltpu.CompilerParams(vmem_limit_bytes=62 * 1024 * 1024),
    )(rows, dpre, bsum, dgrad)


def solution(mesh):
    return jax.shard_map(
        shards,
        mesh=mesh,
        in_specs=(
            P("layer", None, None),
            P("layer", None),
            P("layer", None, ("feat", "par")),
            P("layer", None, ("feat", "par")),
            P("layer", ("feat", "par"), None),
            P("layer", "par", "feat"),
            P("layer", "feat"),
            P("layer", "par", None, "feat", None),
            P(),
        ),
        out_specs=(
            P("layer", "par", "feat"),
            P("layer", "feat"),
            P("layer", "par", None, "feat", None),
        ),
        check_vma=False,
    )
```

```python
import jax
import jax.numpy as jnp
from jax import lax
from jax.experimental import pallas as pl
from jax.experimental.pallas import tpu as pltpu
from jax.sharding import PartitionSpec as P

F32 = jnp.float32
BF16 = jnp.bfloat16
MESH = pl.DeviceIdType.MESH

T = 512
D = 2304
W = D // 2
F = 512
U = 288
RT = 256
Q1 = RT // 4
QH = Q1 // 2
Q2 = RT // 16
CT = 384
BT = 256


def kernel(
    res_h, gain_v, gate_h, up_h, down_h, enc_h, ebias_v, dec_h, dbias_v,
    rows_h, dpre_h, bgrad_v, dgrad_h,
    nrm, rows_t, gate_v, up_v, down_v, hid, enc_v, enc_b, dec_v,
    pre_snd, pre_rcv, pos, act, act_t,
    own, cs_snd, cs_rcv, part, relay, r1_rcv, r2_snd, r2_rcv, fin, tg_snd, tg_rcv, x_snd, x_rcv,
    err, back, bk_snd, bk_rcv, dpre, dg_v,
    ld_sem, out_sem, pre_s, pre_r, cs_s, cs_r, r1_s, r1_r, r2_s, r2_r, tg_s, tg_r, x_s, x_r,
    ga_s, ga_r, gb_s, gb_r, gc_s, gc_r, bk_s, bk_r,
):
    layer = lax.axis_index("layer")
    feat = lax.axis_index("feat")
    par = lax.axis_index("par")
    core = lax.rem(layer, 2)
    x_hi = lax.div(layer, 2)
    zz = lax.div(feat, 4)
    yy = lax.rem(feat, 4)
    low = x_hi == 0
    home = core == par
    away = core != par

    def first_of(role):
        return zz + role * (yy - zz)

    def second_of(role):
        return yy + role * (zz - yy)

    def at(role, first, second):
        return (layer, first * 4 + second + role * 3 * (second - first), par)

    def turn(x, n):
        return lax.rem(x + n, 4)

    sib = layer + 1 - 2 * core
    par_id = (layer, feat, 1 - par)
    sib_id = (sib, feat, par)
    diag_id = (sib, feat, 1 - par)
    xhi_id = (turn(layer, 2), feat, par)

    def remote(src, dst, s, r, to):
        return pltpu.make_async_remote_copy(
            src_ref=src, dst_ref=dst, send_sem=s, recv_sem=r, device_id=to, device_id_type=MESH
        )

    barrier = pltpu.get_barrier_semaphore()
    peers = [par_id, sib_id, diag_id, xhi_id]
    for n in (1, 2, 3):
        peers += [at(0, turn(zz, n), yy), at(0, zz, turn(yy, n))]
    for to in peers:
        pl.semaphore_signal(barrier, inc=1, device_id=to, device_id_type=MESH)

    loads = [
        pltpu.make_async_copy(res_h.at[0], nrm, ld_sem.at[0]),
        pltpu.make_async_copy(enc_h.at[0], enc_v, ld_sem.at[1]),
        pltpu.make_async_copy(gate_h.at[0], gate_v, ld_sem.at[2]),
        pltpu.make_async_copy(up_h.at[0], up_v, ld_sem.at[3]),
        pltpu.make_async_copy(down_h.at[0], down_v, ld_sem.at[4]),
        pltpu.make_async_copy(dec_h.at[0, 0], dec_v, ld_sem.at[5]),
    ]
    for load in loads:
        load.start()

    def loop(count, size, body):
        def run(i, _):
            body(pl.ds(pl.multiple_of(i * size, size), size))
            return 0

        lax.fori_loop(0, count // size, run, 0)

    loads[0].wait()

    def norm_rows(rows):
        x = nrm[rows, :].astype(F32)
        scale = lax.rsqrt(jnp.mean(x * x, axis=-1, keepdims=True) + 1e-6)
        nrm[rows, :] = (x * scale * gain_v[...]).astype(BF16)

    loop(T, 32, norm_rows)
    loads[1].wait()

    def enc_rows(rows):
        enc_b[rows, :] = enc_v[rows, :].astype(BF16)

    loop(W, 128, enc_rows)
    my_cols = pl.ds(pl.multiple_of(par * W, W), W)
    rows_copy = pltpu.make_async_copy(rows_t, rows_h, out_sem.at[2])

    pl.semaphore_wait(barrier, len(peers))
    pre_copy = []
    for c in range(2):
        rows = pl.ds(c * RT, RT)
        partial = jnp.dot(nrm[rows, my_cols], enc_b[...], preferred_element_type=F32)
        pos[rows, :] = partial
        pre_snd[rows, :] = partial.astype(BF16)
        pre_copy.append(remote(pre_snd.at[rows], pre_rcv.at[rows], pre_s.at[c], pre_r.at[c], par_id))
        pre_copy[c].start()

    loads[2].wait()
    loads[3].wait()

    def mlp_rows(rows):
        x = nrm[rows, :]
        g = lax.dot_general(x, gate_v[...], (((1,), (1,)), ((), ())), preferred_element_type=F32)
        u = lax.dot_general(x, up_v[...], (((1,), (1,)), ((), ())), preferred_element_type=F32)
        inner = 0.7978845608028654 * (g + 0.044715 * g * g * g)
        hid[rows, :] = (0.5 * g * (1.0 + jnp.tanh(inner)) * u).astype(BF16)

    def mlp(t):
        mlp_rows(pl.ds(t * RT, RT))
        for h in range(2):

            def down_cols(local):
                cols = pl.ds(pl.multiple_of(local.start + h * W, CT), CT)
                part[2 * t + h, :, local] = jnp.dot(
                    hid[t * RT : (t + 1) * RT, :], down_v[:, cols], preferred_element_type=F32
                ).astype(BF16)

            loop(W, CT, down_cols)

            @pl.when(away)
            def _():
                ring_start(2 * t + h)

    def role_of(u):
        return u % 2 if u < 4 else core

    def half_rows(blk, half):
        return pl.ds(pl.multiple_of(blk * Q1 + half * QH, QH), QH)

    def ring(u, m):
        role = role_of(u)
        i, k = first_of(role), second_of(role)
        up1, down1, far = turn(i, 1), turn(i, 3), turn(i, 2)
        right, left = at(role, up1, k), at(role, down1, k)
        src, to = [
            (lambda: part.at[u, half_rows(far, 0)], right),
            (lambda: part.at[u, half_rows(far, 1)], left),
            (lambda: part.at[u, half_rows(up1, 1)], right),
            (lambda: part.at[u, half_rows(down1, 0)], left),
            (lambda: relay.at[u, 0], right),
            (lambda: relay.at[u, 1], left),
        ][m]
        return remote(src(), r1_rcv.at[u, m], r1_s.at[u, m], r1_r.at[u, m], to)

    def ring_start(u):
        for m in range(4):
            ring(u, m).start()

    def ring_relay(u):
        i = first_of(role_of(u))
        for m, blk in ((0, turn(i, 1)), (1, turn(i, 3))):
            ring(u, m).wait_recv()
            relay[u, m] = (r1_rcv[u, m].astype(F32) + part[u, half_rows(blk, m), :].astype(F32)).astype(BF16)
            ring(u, 4 + m).start()

    def second_copy(u, n):
        role = role_of(u)
        to = at(role, first_of(role), turn(second_of(role), n))
        return remote(r2_snd.at[u, n - 1], r2_rcv.at[u, n - 1], r2_s.at[u, n - 1], r2_r.at[u, n - 1], to)

    def second_start(u):
        role = role_of(u)
        i, k = first_of(role), second_of(role)
        for m in (2, 3, 4, 5):
            ring(u, m).wait_recv()

        def piece(q):
            half = lax.div(q, 2)
            here = pl.ds(pl.multiple_of(lax.rem(q, 2) * Q2, Q2), Q2)
            rows = pl.ds(pl.multiple_of(i * Q1 + q * Q2, Q2), Q2)
            return (
                part[u, rows, :].astype(F32)
                + r1_rcv[u, 3 - half, here, :].astype(F32)
                + r1_rcv[u, 4 + half, here, :].astype(F32)
            )

        for n in (1, 2, 3):
            r2_snd[u, n - 1] = piece(turn(k, n)).astype(BF16)
            second_copy(u, n).start()
        fin[u] = piece(k)

    def second_end(u):
        for n in (1, 2, 3):
            second_copy(u, n).wait_recv()
        total = fin[u]
        for n in range(3):
            total = total + r2_rcv[u, n].astype(F32)
        fin[u] = total

    live0 = par >= layer
    live1 = 2 + par >= layer
    half_cols = pl.ds(pl.multiple_of(core * W, W), W)

    def activate(c):
        pre_copy[c].wait_recv()

        def act_rows(rows):
            rows = pl.ds(pl.multiple_of(c * RT + rows.start, 32), 32)
            p = jnp.maximum(pos[rows, :] + pre_rcv[rows, :].astype(F32) + ebias_v[...], 0.0)
            pos[rows, :] = p
            act[rows, :] = (p * p).astype(BF16)

        loop(RT, 32, act_rows)

    def core_copy(j, r):
        rows = pl.ds(r * RT, RT)
        return remote(cs_snd.at[j, rows], cs_rcv.at[j, rows], cs_s.at[j, r], cs_r.at[j, r], sib_id)

    def recon(j, r):
        live = (live1 if j == 1 else live0).astype(F32)
        ours = jnp.logical_and(home, x_hi == j).astype(F32)
        rows = pl.ds(r * RT, RT)
        x = act[rows, :]

        def tile(half, local):
            cols = pl.ds(pl.multiple_of(half * W + local.start, CT), CT)
            out = jnp.dot(x, dec_v[j, :, cols], preferred_element_type=F32)
            return out * live - part[2 * r + half, :, local].astype(F32) * ours

        def for_sibling(local):
            cs_snd[j, rows, local] = tile(1 - core, local).astype(BF16)

        def for_self(local):
            own[j, rows, local] = tile(core, local)

        loop(W, CT, for_sibling)
        core_copy(j, r).start()
        loop(W, CT, for_self)

    def chip_sum(j, t):
        core_copy(j, t).wait_recv()

        def add_rows(rows):
            whole = pl.ds(pl.multiple_of(t * RT + rows.start, 32), 32)
            part[unit(j, t), rows, :] = (own[j, whole, :] + cs_rcv[j, whole, :].astype(F32)).astype(BF16)

        loop(RT, 32, add_rows)
        ring_start(unit(j, t))

    def unit(j, t):
        return 5 + 2 * t - j

    def tg_par(t):
        return remote(tg_snd.at[t, 0], tg_rcv.at[t], tg_s.at[t, 0], tg_r.at[t], par_id)

    def tg_diag(t):
        return remote(tg_snd.at[t, 1], tg_rcv.at[t], tg_s.at[t, 1], tg_r.at[t], diag_id)

    def x_copy(t):
        return remote(x_snd.at[t], x_rcv.at[t], x_s.at[t], x_r.at[t], xhi_id)

    a, b = first_of(core), second_of(core)

    def piece_rows(t):
        return pl.ds(pl.multiple_of(t * RT + a * Q1 + b * Q2, Q2), Q2)

    def write_error(j, t, total):
        bias = dbias_v[pl.ds(2 * j + par, 1), half_cols]
        err[core, j, piece_rows(t), :] = ((total + bias) * 0.0625).astype(BF16)

    def take_target(j, t):
        tg_par(t).wait_recv()
        fin[unit(j, t)] = fin[unit(j, t)] - tg_rcv[t].astype(F32)

    def block(t, first):
        return pl.ds(pl.multiple_of(t * RT + first * Q1, Q1), Q1)

    def half_block(t, first, half):
        return pl.ds(pl.multiple_of(t * RT + first * Q1 + half * QH, QH), QH)

    def gather_a(j, t, n):
        piece = err.at[core, j, piece_rows(t)]
        return remote(piece, piece, ga_s.at[2 * j + t, n - 1], ga_r.at[2 * j + t, n - 1], at(core, a, turn(b, n)))

    def gather_b(j, t, m):
        rows, n = [
            (block(t, a), 1),
            (block(t, a), 3),
            (half_block(t, turn(a, 3), 0), 1),
            (half_block(t, turn(a, 1), 1), 3),
        ][m]
        piece = err.at[core, j, rows]
        return remote(piece, piece, gb_s.at[2 * j + t, m], gb_r.at[2 * j + t, m], at(core, turn(a, n), b))

    def gather_c(j, t, n):
        piece = err.at[core, j, block(t, turn(a, n))]
        return remote(piece, piece, gc_s.at[2 * j + t, n], gc_r.at[2 * j + t, n], sib_id)

    def gather_1(j, t):
        for n in (2, 1, 3):
            gather_a(j, t, n).start()

    def gather_2(j, t):
        for n in (1, 3, 2):
            gather_a(j, t, n).wait_recv()
        gather_b(j, t, 0).start()
        gather_b(j, t, 1).start()
        gather_c(j, t, 0).start()

    def gather_3(j, t):
        gather_b(j, t, 0).wait_recv()
        gather_b(j, t, 2).start()
        gather_c(j, t, 3).start()
        gather_b(j, t, 1).wait_recv()
        gather_b(j, t, 3).start()
        gather_c(j, t, 1).start()

    def gather_4(j, t):
        gather_b(j, t, 2).wait_recv()
        gather_b(j, t, 3).wait_recv()
        gather_c(j, t, 2).start()

    def wait_error(j, t):
        for n in (0, 1, 3, 2):
            gather_c(j, t, n).wait_recv()

    def each(stage, t):
        stage(1, t)

        @pl.when(low)
        def _():
            stage(0, t)

    def target(stage, t):
        @pl.when(away)
        def _():
            for h in range(2):
                stage(2 * t + h)

    def send_target(t):
        @pl.when(away)
        def _():
            second_end(2 * t)
            second_end(2 * t + 1)
            tg_snd[t, 0] = fin[2 * t + core].astype(BF16)
            tg_snd[t, 1] = fin[2 * t + 1 - core].astype(BF16)
            tg_par(t).start()
            tg_diag(t).start()

    def send_slot_1(t):
        second_end(unit(1, t))

        @pl.when(jnp.logical_not(low))
        def _():
            take_target(1, t)

        x_snd[t] = fin[unit(1, t)].astype(BF16)
        x_copy(t).start()

    def error_1(t):
        x_copy(t).wait_recv()
        write_error(1, t, fin[unit(1, t)] + x_rcv[t].astype(F32))
        gather_1(1, t)

    def error_0(t):
        @pl.when(low)
        def _():
            second_end(unit(0, t))
            take_target(0, t)
            write_error(0, t, fin[unit(0, t)])
            gather_1(0, t)

    def relay_of(j, t):
        ring_relay(unit(j, t))

    def second_of_unit(j, t):
        second_start(unit(j, t))

    loads[4].wait()
    mlp(0)
    activate(0)
    loads[5].wait()
    each(recon, 0)
    target(ring_relay, 0)
    each(chip_sum, 0)
    mlp(1)
    target(second_start, 0)
    each(relay_of, 0)
    activate(1)
    each(recon, 1)
    each(second_of_unit, 0)
    target(ring_relay, 1)
    send_target(0)
    each(chip_sum, 1)
    send_slot_1(0)
    error_0(0)
    each(relay_of, 1)
    target(second_start, 1)
    error_1(0)

    each(second_of_unit, 1)
    send_target(1)
    each(gather_2, 0)
    send_slot_1(1)
    error_0(1)
    error_1(1)
    each(gather_3, 0)
    each(gather_2, 1)
    act_t[...] = act[...].T
    for n in range(W // CT):
        cols = pl.ds(pl.multiple_of(par * W + n * CT, 128), CT)
        rows_t[pl.ds(n * CT, CT), :] = nrm[:, cols].T
    rows_copy.start()

    each(gather_4, 0)
    each(wait_error, 0)

    def back_tile(j, rows):
        out = None
        for h in range(2):
            term = lax.dot_general(
                err[h, j, rows, :], dec_v[j, :, pl.ds(h * W, W)], (((1,), (1,)), ((), ())),
                preferred_element_type=F32,
            )
            out = term if out is None else out + term
        return out

    def dec_grad(j):
        for h in range(2):

            def grad_cols(local):
                cols = pl.ds(pl.multiple_of(local.start + h * W, CT), CT)
                dg_v[j, :, cols] = jnp.dot(
                    act_t[...], err[h, j, :, local], preferred_element_type=F32
                ).astype(BF16)

            loop(W, CT, grad_cols)

    def no_dec_grad(j):
        def zero_rows(rows):
            dg_v[j, rows, :] = jnp.zeros((32, D), BF16)

        loop(F, 32, zero_rows)

    outs = [pltpu.make_async_copy(dg_v.at[j], dgrad_h.at[j], out_sem.at[j]) for j in range(2)]

    bk_copy = []

    def back_rows(r):
        rows = pl.ds(r * BT, BT)

        @pl.when(live1)
        def _():
            back[rows, :] = back_tile(1, rows)

        @pl.when(jnp.logical_not(live1))
        def _():
            back[rows, :] = jnp.zeros((BT, F), F32)

        @pl.when(live0)
        def _():
            back[rows, :] += back_tile(0, rows)

        bk_snd[rows, :] = back[rows, :].astype(BF16)
        bk_copy.append(remote(bk_snd.at[rows], bk_rcv.at[rows], bk_s.at[r], bk_r.at[r], par_id))
        bk_copy[r].start()

    each(gather_3, 1)
    for r in range(T // BT // 2):
        back_rows(r)
    each(gather_4, 1)
    each(wait_error, 1)
    for r in range(T // BT // 2, T // BT):
        back_rows(r)

    for j, live in ((1, live1), (0, live0)):

        @pl.when(live)
        def _():
            dec_grad(j)

        @pl.when(jnp.logical_not(live))
        def _():
            no_dec_grad(j)

        outs[j].start()

    bgrad_v[...] = jnp.zeros((1, F), F32)
    for r in range(T // BT):
        bk_copy[r].wait_recv()

        def dpre_rows(rows):
            rows = pl.ds(pl.multiple_of(r * BT + rows.start, 32), 32)
            d = (back[rows, :] + bk_rcv[rows, :].astype(F32)) * 2.0 * pos[rows, :]
            dpre[rows, :] = d.astype(BF16)
            bgrad_v[...] += jnp.sum(d, axis=0, keepdims=True)

        loop(BT, 32, dpre_rows)

    last = pltpu.make_async_copy(dpre, dpre_h, out_sem.at[3])
    last.start()

    for copy in pre_copy + bk_copy:
        copy.wait_send()

    def drain(u):
        for m in range(6):
            ring(u, m).wait_send()
        for n in (1, 2, 3):
            second_copy(u, n).wait_send()

    def drain_slot(j, t):
        drain(unit(j, t))
        core_copy(j, t).wait_send()
        for n in (1, 2, 3):
            gather_a(j, t, n).wait_send()
        for n in range(4):
            gather_b(j, t, n).wait_send()
            gather_c(j, t, n).wait_send()

    for t in range(2):
        each(drain_slot, t)
        target(drain, t)
        x_copy(t).wait_send()

    @pl.when(away)
    def _():
        for t in range(2):
            tg_par(t).wait_send()
            tg_diag(t).wait_send()

    for copy in outs:
        copy.wait()
    rows_copy.wait()
    last.wait()


def finish_kernel(
    rows_h, dpre_h, bsum_v, dgrad_h, egrad_h, bgrad_v, dout_h, rows_v, dpre_v, eg_v, dg_v, ld_sem, in_sem, out_sem, cp_sem
):
    loads = [
        pltpu.make_async_copy(dpre_h, dpre_v, ld_sem.at[0]),
        pltpu.make_async_copy(rows_h, rows_v, ld_sem.at[1]),
    ]
    here = [(j, pl.ds(r * RT, RT)) for j in range(2) for r in range(2)]
    arrive = [pltpu.make_async_copy(dgrad_h.at[p], dg_v.at[p], in_sem.at[n]) for n, p in enumerate(here)]
    leave = [pltpu.make_async_copy(dg_v.at[p], dout_h.at[(0, 0) + p], cp_sem.at[n]) for n, p in enumerate(here)]
    for copy in loads + arrive:
        copy.start()
    for copy in loads:
        copy.wait()
    bgrad_v[...] = bsum_v[...]
    outs = []
    for n in range(W // CT):
        rows = pl.ds(n * CT, CT)
        eg_v[rows, :] = jnp.dot(rows_v[rows, :], dpre_v[...], preferred_element_type=F32)
        outs.append(pltpu.make_async_copy(eg_v.at[rows], egrad_h.at[0, rows], out_sem.at[n]))
        outs[n].start()
        arrive[n].wait()
        leave[n].start()
    arrive[3].wait()
    leave[3].start()
    for copy in outs + leave:
        copy.wait()


def shards(
    residual, norm_gain, gate_weight, up_weight, down_weight, enc_weight, enc_bias, dec_weight, dec_bias
):
    any_spec = pl.BlockSpec(memory_space=pl.ANY)
    vmem = pl.BlockSpec(memory_space=pltpu.VMEM)
    dma = pltpu.SemaphoreType.DMA

    def pair(*shape):
        return [dma(shape), dma(shape)]

    scratch = [
        pltpu.VMEM((T, D), BF16),
        pltpu.VMEM((W, T), BF16),
        pltpu.VMEM((U, D), BF16),
        pltpu.VMEM((U, D), BF16),
        pltpu.VMEM((U, D), BF16),
        pltpu.VMEM((T, U), BF16),
        pltpu.VMEM((W, F), F32),
        pltpu.VMEM((W, F), BF16),
        pltpu.VMEM((2, F, D), BF16),
        pltpu.VMEM((T, F), BF16),
        pltpu.VMEM((T, F), BF16),
        pltpu.VMEM((T, F), F32),
        pltpu.VMEM((T, F), BF16),
        pltpu.VMEM((F, T), BF16),
        pltpu.VMEM((2, T, W), F32),
        pltpu.VMEM((2, T, W), BF16),
        pltpu.VMEM((2, T, W), BF16),
        pltpu.VMEM((8, RT, W), BF16),
        pltpu.VMEM((8, 2, QH, W), BF16),
        pltpu.VMEM((8, 6, QH, W), BF16),
        pltpu.VMEM((8, 3, Q2, W), BF16),
        pltpu.VMEM((8, 3, Q2, W), BF16),
        pltpu.VMEM((8, Q2, W), F32),
        pltpu.VMEM((2, 2, Q2, W), BF16),
        pltpu.VMEM((2, Q2, W), BF16),
        pltpu.VMEM((2, Q2, W), BF16),
        pltpu.VMEM((2, Q2, W), BF16),
        pltpu.VMEM((2, 2, T, W), BF16),
        pltpu.VMEM((T, F), F32),
        pltpu.VMEM((T, F), BF16),
        pltpu.VMEM((T, F), BF16),
        pltpu.VMEM((T, F), BF16),
        pltpu.VMEM((2, F, D), BF16),
        dma((6,)), dma((4,)),
    ]
    scratch += pair(2) + pair(2, 2) + pair(8, 6) + pair(8, 3)
    scratch += [dma((2, 2)), dma((2,))] + pair(2)
    scratch += pair(4, 3) + pair(4, 4) + pair(4, 4) + pair(T // BT)
    rows, dpre, bsum, dgrad = pl.pallas_call(
        kernel,
        out_shape=(
            jax.ShapeDtypeStruct((W, T), BF16),
            jax.ShapeDtypeStruct((T, F), BF16),
            jax.ShapeDtypeStruct((1, F), F32),
            jax.ShapeDtypeStruct((2, F, D), BF16),
        ),
        in_specs=[any_spec, vmem, any_spec, any_spec, any_spec, any_spec, vmem, any_spec, vmem],
        out_specs=(any_spec, any_spec, vmem, any_spec),
        scratch_shapes=scratch,
        compiler_params=pltpu.CompilerParams(
            collective_id=0, has_side_effects=True, vmem_limit_bytes=62 * 1024 * 1024
        ),
    )(
        residual,
        norm_gain,
        jnp.swapaxes(gate_weight, 1, 2),
        jnp.swapaxes(up_weight, 1, 2),
        down_weight,
        enc_weight,
        enc_bias,
        dec_weight,
        dec_bias,
    )
    return pl.pallas_call(
        finish_kernel,
        out_shape=(
            jax.ShapeDtypeStruct((1, W, F), F32),
            jax.ShapeDtypeStruct((1, F), F32),
            jax.ShapeDtypeStruct((1, 1, 2, F, D), BF16),
        ),
        in_specs=[any_spec, any_spec, vmem, any_spec],
        out_specs=(any_spec, vmem, any_spec),
        scratch_shapes=[
            pltpu.VMEM((W, T), BF16),
            pltpu.VMEM((T, F), BF16),
            pltpu.VMEM((W, F), F32),
            pltpu.VMEM((2, F, D), BF16),
            dma((2,)),
            dma((4,)),
            dma((W // CT,)),
            dma((4,)),
        ],
        compiler_params=pltpu.CompilerParams(vmem_limit_bytes=62 * 1024 * 1024),
    )(rows, dpre, bsum, dgrad)


def solution(mesh):
    return jax.shard_map(
        shards,
        mesh=mesh,
        in_specs=(
            P("layer", None, None),
            P("layer", None),
            P("layer", None, ("feat", "par")),
            P("layer", None, ("feat", "par")),
            P("layer", ("feat", "par"), None),
            P("layer", "par", "feat"),
            P("layer", "feat"),
            P("layer", "par", None, "feat", None),
            P(),
        ),
        out_specs=(
            P("layer", "par", "feat"),
            P("layer", "feat"),
            P("layer", "par", None, "feat", None),
        ),
        check_vma=False,
    )
```
